32 devices in a mesh: row: 8 (over z, x), col: 4 (over y, core).
Axes of the slice: x: 2, y: 2, z: 4, core: 2. Of those that a mesh axis runs over, the one named last changes fastest.
Arguments:
- start_block: float32 [8, 32768], P(None, ('row', 'col')), may hold values from -6 to 6
- blocks: bfloat16 [8, 4, 128, 128, 128], P('row', 'col'), as said below
- block_rows: int32 [8, 4, 128], P(None, 'col'), may hold values from 0 to 31, as said below
- block_cols: int32 [8, 4, 128], P(None, 'col'), may hold values from 0 to 63, as said below
- counts: int32 [8, 4], replicated, may hold values from 1 to 128, as said below
Outputs:
- next_block: float32 [8, 32768], P(None, ('row', 'col'))
- tridiagonal: float32 [16, 16], replicated
The draws below stay inside these ranges and needn't reach their ends.
Inputs may be any that keep to these rules, and one draw needn't show every extreme that they name: `block_rows`: entries of each tile are local block rows below 32; within a tile the used slots name distinct blocks whose global row block is at or after the global column block; slots at or after counts are 0 and not part of H. `block_cols`: local block columns below 64, paired with block_rows; unused slots are 0. `counts`: some tile holds exactly 128 blocks in every draw. Blocks whose global row and column blocks agree are symmetric.
All inputs are finite; a program needn't handle non-finite values.
Results may differ from the reference program's by a relative error of at most 0.0048.
Values may be sent and summed in bfloat16 or wider, within the bound.
No kernel may reach another device: no remote copies, remote signals or barrier semaphores. Data moves between devices by JAX's collectives and lax.ppermute only.
A program may use at most 64 MiB of HBM per device.

```python
import jax
import jax.numpy as jnp
from jax import lax

BS = 128
K = 8
ITERS = 2
M = 8
MAXB = 128
VP = 1024
NV = 32768
N_ROW = 8
N_COL = 4


def layout(key):
    base = jax.random.fold_in(key, 11)
    row_blocks = N_COL * M
    col_blocks = N_ROW * M
    pairs = row_blocks * col_blocks
    pair_ids = jnp.arange(pairs, dtype=jnp.int32)
    local_row = pair_ids // col_blocks
    local_col = pair_ids % col_blocks
    grid_row = jnp.arange(N_ROW, dtype=jnp.int32)[:, None, None]
    grid_col = jnp.arange(N_COL, dtype=jnp.int32)[None, :, None]
    global_row = grid_row * row_blocks + local_row[None, None, :]
    global_col = (local_col[None, None, :] // M * N_COL + grid_col) * M + local_col[None, None, :] % M
    allowed = global_row >= global_col
    candidates = jnp.sum(allowed.astype(jnp.int32), axis=-1)
    chosen_col = jax.random.randint(jax.random.fold_in(base, 1), (), 0, N_COL)
    anchor_count = candidates[N_ROW - 1, chosen_col]
    jitter = jax.random.randint(jax.random.fold_in(base, 2), (N_ROW, N_COL), 0, MAXB // 8 + 2)
    jitter = jnp.where(grid_row[:, :, 0] == N_ROW - 1, 0, jitter)
    target = candidates * MAXB // anchor_count - jitter
    counts = jnp.clip(target, 1, jnp.minimum(candidates, MAXB)).astype(jnp.int32)
    limit = 2 ** 30 // pairs
    scores = jax.random.randint(jax.random.fold_in(base, 3), (N_ROW, N_COL, pairs), 0, limit) * pairs + pair_ids[None, None, :]
    scores = jnp.where(allowed, scores, scores + 2 ** 30)
    order = jnp.argsort(scores, axis=-1, stable=True)[..., :MAXB]
    slot_ids = jnp.arange(MAXB, dtype=jnp.int32)
    used = slot_ids[None, None, :] < counts[..., None]
    rows = jnp.where(used, local_row[order], 0).astype(jnp.int32)
    cols = jnp.where(used, local_col[order], 0).astype(jnp.int32)
    return (rows, cols, counts)


def draw_block_rows(key, part):
    rows, cols, counts = layout(key)
    return rows


def draw_block_cols(key, part):
    rows, cols, counts = layout(key)
    return cols


def draw_counts(key, part):
    rows, cols, counts = layout(key)
    return counts


def draw_blocks(key, part):
    rows, cols, counts = layout(key)
    grid_row = jnp.arange(N_ROW, dtype=jnp.int32)[:, None, None]
    grid_col = jnp.arange(N_COL, dtype=jnp.int32)[None, :, None]
    global_row = grid_row * (N_COL * M) + rows
    global_col = (cols // M * N_COL + grid_col) * M + cols % M
    diagonal = global_row == global_col
    shape = (N_ROW, N_COL, MAXB, BS, BS)
    noise_key = jax.random.fold_in(key, 5)
    scale = (M / (MAXB * BS)) ** 0.5
    values = jax.random.normal(noise_key, shape, jnp.float32)
    values = values * scale
    mirrored = 0.5 * (values + jnp.swapaxes(values, -1, -2))
    return jnp.where(diagonal[..., None, None], mirrored, values).astype(jnp.bfloat16)


def steps_of(stream_key, extent, shards, smallest, top_value):
    loudness, own = 1.0, jax.random.fold_in(stream_key, 6)
    for dim, shards_of in shards:
        draws = jnp.exp(jax.random.uniform(jax.random.fold_in(own, dim), (shards_of,), jnp.float32, smallest / len(shards), top_value / len(shards)))
        loudness = loudness * jnp.repeat(draws, extent[dim] // shards_of).reshape([-1 if axis == dim else 1 for axis in range(len(extent))])
    return loudness


def centred(own_key, shape, spread, most, cuts=(), kind=jnp.bfloat16):
    gain = steps_of(own_key, shape, cuts, -0.22, 0.18) if cuts else 1.0
    result = jax.random.normal(own_key, shape, jnp.float32) * spread * gain
    return jnp.minimum(jnp.maximum(result, -most), most).astype(kind)


def setup_inputs(seed: int = 0) -> dict:
    arg_keys = jax.random.split(jax.random.key(seed), 6)
    start_block = centred(arg_keys[0], (K, NV), 1.0, 6.0, ((1, 32),), jnp.float32)
    blocks = draw_blocks(jax.random.fold_in(arg_keys[5], 71), 0)
    block_rows = draw_block_rows(jax.random.fold_in(arg_keys[5], 71), 0)
    block_cols = draw_block_cols(jax.random.fold_in(arg_keys[5], 71), 0)
    counts = draw_counts(jax.random.fold_in(arg_keys[5], 71), 0)
    return dict(start_block=start_block, blocks=blocks, block_rows=block_rows, block_cols=block_cols, counts=counts)


def product(half, blocks, block_rows, block_cols, counts):
    vectors = half.shape[0]
    whole = half.astype(jnp.float32).reshape(vectors, N_ROW, N_COL, VP)
    row_blocks = N_COL * M
    col_blocks = N_ROW * M
    slot_ids = jnp.arange(MAXB, dtype=jnp.int32)

    def visit(tile_index, total):
        tile_row = (tile_index // N_COL).astype(jnp.int32)
        tile_col = (tile_index % N_COL).astype(jnp.int32)
        tile_data = blocks[tile_row, tile_col].astype(jnp.float32)
        row_ids = block_rows[tile_row, tile_col].astype(jnp.int32)
        col_ids = block_cols[tile_row, tile_col].astype(jnp.int32)
        is_live = slot_ids < counts[tile_row, tile_col]
        row_vector = lax.dynamic_index_in_dim(whole, tile_row, 1, False).reshape(vectors, row_blocks, BS)
        col_vector = lax.dynamic_index_in_dim(whole, tile_col, 2, False).reshape(vectors, col_blocks, BS)
        global_row = tile_row * row_blocks + row_ids
        global_col = (col_ids // M * N_COL + tile_col) * M + col_ids % M
        mirror = is_live & (global_row != global_col)
        direct = jnp.einsum('gij,kgj->kgi', tile_data, col_vector[:, col_ids])
        turned = jnp.einsum('gji,kgj->kgi', tile_data, row_vector[:, row_ids])
        direct = jnp.where(is_live[None, :, None], direct, 0.0)
        turned = jnp.where(mirror[None, :, None], turned, 0.0)
        row_out = jnp.zeros((vectors, row_blocks, BS), jnp.float32).at[:, row_ids].add(direct)
        col_out = jnp.zeros((vectors, col_blocks, BS), jnp.float32).at[:, col_ids].add(turned)
        row_now = lax.dynamic_index_in_dim(total, tile_row, 1, False) + row_out.reshape(vectors, N_COL, VP)
        total = lax.dynamic_update_index_in_dim(total, row_now, tile_row, 1)
        col_now = lax.dynamic_index_in_dim(total, tile_col, 2, False) + col_out.reshape(vectors, N_ROW, VP)
        total = lax.dynamic_update_index_in_dim(total, col_now, tile_col, 2)
        return total
    total = lax.fori_loop(0, N_ROW * N_COL, visit, jnp.zeros((vectors, N_ROW, N_COL, VP), jnp.float32))
    return total.reshape(vectors, N_ROW * N_COL * VP)

def reference(start_block, blocks, block_rows, block_cols, counts):
    highest = lax.Precision.HIGHEST
    factor = jnp.linalg.cholesky(jnp.dot(start_block, start_block.T, precision=highest))
    current = lax.linalg.triangular_solve(factor, start_block, left_side=True, lower=True)
    previous = current
    prev_factor = factor
    diagonals = []
    couplings = []
    for step_index in range(ITERS):
        image = product(current.astype(jnp.bfloat16), blocks, block_rows, block_cols, counts)
        if step_index > 0:
            image = image - jnp.dot(prev_factor.T, previous, precision=highest)
        projection = jnp.dot(current, image.T, precision=highest)
        image = image - jnp.dot(projection.T, current, precision=highest)
        gram = jnp.dot(image, image.T, precision=highest)
        factor = jnp.linalg.cholesky(gram)
        following = lax.linalg.triangular_solve(factor, image, left_side=True, lower=True)
        diagonals.append(projection)
        couplings.append(factor)
        previous, prev_factor, current = (current, factor, following)
    tri_size = ITERS * K
    tridiagonal = jnp.zeros((tri_size, tri_size), jnp.float32)
    for step_index in range(ITERS):
        low = step_index * K
        tridiagonal = tridiagonal.at[low:low + K, low:low + K].set(diagonals[step_index])
        if step_index + 1 < ITERS:
            tridiagonal = tridiagonal.at[low:low + K, low + K:low + 2 * K].set(couplings[step_index])
            tridiagonal = tridiagonal.at[low + K:low + 2 * K, low:low + K].set(couplings[step_index].T)
    return (current * jnp.sqrt(jnp.float32(NV)), tridiagonal)
```

```python
import functools
import math

import jax
import jax.numpy as jnp
from jax import lax
from jax.experimental import pallas as pl
from jax.experimental.pallas import tpu as pltpu
from jax.sharding import PartitionSpec as P

ITERS = 2
LANES = 128
GROUP = 16
DOWN = 2.0**-6
UP = 2.0**6

VMEM = pl.BlockSpec(memory_space=pltpu.VMEM)
SMEM = pl.BlockSpec(memory_space=pltpu.SMEM)
ANY = pl.BlockSpec(memory_space=pl.ANY)
f32 = jnp.float32


def split_terms(x):
    coarse = x.astype(jnp.bfloat16).astype(f32)
    return jnp.concatenate([coarse, x - coarse], axis=0).astype(jnp.bfloat16)


def lane_ids(k):
    return lax.broadcasted_iota(jnp.int32, (k, LANES), 1)


def row_ids(k, width):
    return lax.broadcasted_iota(jnp.int32, (k, width), 0)


def inner(left, right):
    k, width = left.shape
    row, lane = row_ids(k, LANES), lane_ids(k)
    result = jnp.zeros((k, LANES), f32)
    for turn in range(k):
        turned = right if turn == 0 else pltpu.roll(right, turn, 0)
        product = left * turned
        total = product[:, :LANES]
        for low in range(LANES, width, LANES):
            total = total + product[:, low : low + LANES]
        value = jnp.sum(total, axis=1, keepdims=True)
        spot = lane == jnp.where(row >= turn, row - turn, row - turn + k)
        result = jnp.where(spot, value, result)
    return result


def matmul_small(square, tall, transposed=False):
    k, width = tall.shape
    if transposed:
        square = transpose_small(square)
    result = jnp.zeros((k, width), f32)
    for i in range(k):
        result = result + square[:, i : i + 1] * tall[i : i + 1, :]
    return result


def transpose_small(square):
    k = square.shape[0]
    row, lane = row_ids(k, LANES), lane_ids(k)
    result = jnp.zeros((k, LANES), f32)
    for i in range(k):
        line = jnp.sum(
            jnp.where(lane == row_ids(k, LANES), square[:, i : i + 1], 0.0), axis=0, keepdims=True
        )
        result = jnp.where(row == i, line, result)
    return result


def eliminate(gram, tall):
    k, width = tall.shape
    row_small, row_tall = row_ids(k, LANES), row_ids(k, width)
    for i in range(k):
        column = gram[:, i : i + 1]
        scale = 1.0 / jnp.sqrt(gram[i : i + 1, i : i + 1])
        factor = column * scale
        line_small = gram[i : i + 1, :] * scale
        line_tall = tall[i : i + 1, :] * scale
        gram = jnp.where(
            row_small < i,
            gram,
            jnp.where(row_small == i, line_small, gram - factor * line_small),
        )
        tall = jnp.where(
            row_tall < i,
            tall,
            jnp.where(row_tall == i, line_tall, tall - factor * line_tall),
        )
    lane = lane_ids(k)
    upper = jnp.where((lane >= row_small) & (lane < k), gram, 0.0)
    return upper, tall


def own_place():
    return lax.axis_index("row"), lax.axis_index("col")


def start_blocks(count, blocks, held, arrived):
    slots = blocks.shape[0]
    for part in range(slots // GROUP):

        @pl.when(part * GROUP < count)
        def _():
            rows = pl.ds(part * GROUP, GROUP)
            pltpu.make_async_copy(blocks.at[rows], held.at[rows], arrived.at[part]).start()


def each_group(count, blocks, held, arrived, work):
    def step(part, carry):
        rows = pl.ds(part * GROUP, GROUP)
        pltpu.make_async_copy(blocks.at[rows], held.at[rows], arrived.at[part]).wait()
        work(part * GROUP)
        return carry

    lax.fori_loop(0, (count + GROUP - 1) // GROUP, step, 0)


def turned_kernel(grid, scale, pairs, *refs):
    grid_rows, grid_cols, piece_blocks = grid
    counts, block_rows, block_cols, blocks = refs[:4]
    pieces = refs[4 : 4 + grid_cols]
    others = refs[4 + grid_cols : 4 + 2 * grid_cols] if pairs else None
    sent, taken, total, held, arrived = refs[-5:]
    r, c = own_place()
    count = counts[r, c]
    start_blocks(count, blocks, held, arrived)
    vectors = pieces[0].shape[0]
    trash = grid_rows * piece_blocks
    for shift in range(grid_cols):
        place = lax.rem(c - shift + grid_cols, grid_cols) * piece_blocks
        for b in range(piece_blocks):
            x = pieces[shift][:, b * LANES : (b + 1) * LANES]
            taken[place + b] = split_terms(x * scale if scale != 1.0 else x)
    total[...] = jnp.zeros_like(total)

    def work(first):
        for g in range(GROUP):
            slot = first + g
            rid, cid = block_rows[r, slot], block_cols[r, slot]
            inside = rid - c * piece_blocks
            same = (inside == cid - r * piece_blocks) & (inside >= 0) & (inside < piece_blocks)
            goal = jnp.where((slot < count) & jnp.logical_not(same), cid, trash)
            y = jnp.dot(taken[rid], held[slot], preferred_element_type=f32)
            total[goal] += y[:vectors] + y[vectors:]

    each_group(count, blocks, held, arrived, work)
    gram = jnp.zeros((vectors, LANES), f32)
    for shift in range(grid_cols):
        p = pieces[shift][...]
        if pairs:
            gram = gram + inner(others[shift][...], p) + pltpu.roll(inner(p, p), vectors, 1)
        else:
            gram = gram + inner(p, p)
    for piece in range(grid_rows):
        for b in range(piece_blocks):
            sent[piece, :, b * LANES : (b + 1) * LANES] = total[piece * piece_blocks + b]
        sent[piece, :, piece_blocks * LANES :] = gram


def direct_kernel(grid, scale, *refs):
    grid_rows, grid_cols, piece_blocks = grid
    counts, block_rows, block_cols, blocks, gathered = refs[:5]
    outs = refs[5 : 5 + grid_cols]
    taken, total, held, arrived = refs[-4:]
    r, c = own_place()
    count = counts[r, c]
    start_blocks(count, blocks, held, arrived)
    vectors = gathered.shape[1]
    trash = grid_cols * piece_blocks
    for piece in range(grid_rows):
        for b in range(piece_blocks):
            x = gathered[piece, :, b * LANES : (b + 1) * LANES]
            taken[piece * piece_blocks + b] = split_terms(x * scale if scale != 1.0 else x)
    total[...] = jnp.zeros_like(total)

    def work(first):
        for g in range(GROUP):
            slot = first + g
            rid, cid = block_rows[r, slot], block_cols[r, slot]
            goal = jnp.where(slot < count, rid, trash)
            y = lax.dot_general(
                taken[cid], held[slot], (((1,), (1,)), ((), ())), preferred_element_type=f32
            )
            total[goal] += y[:vectors] + y[vectors:]

    each_group(count, blocks, held, arrived, work)
    for shift in range(grid_cols):
        place = lax.rem(c + shift, grid_cols) * piece_blocks
        for b in range(piece_blocks):
            outs[shift][:, b * LANES : (b + 1) * LANES] = total[place + b]


def summed(received, parts):
    piece_len = parts[0].shape[1]
    whole = received[0]
    for i in range(1, received.shape[0]):
        whole = whole + received[i]
    image = whole[:, :piece_len]
    for part in parts:
        image = image + part[...]
    return image, whole[:, piece_len:]


def first_kernel(grid, *refs):
    grid_rows, grid_cols, _ = grid
    received = refs[0]
    parts = refs[1 : 1 + grid_cols]
    start, image_out, copies, basis, inverse = refs[1 + grid_cols :]
    image, gram = summed(received, parts)
    k, width = image.shape
    unit = (lane_ids(k) == row_ids(k, LANES)).astype(f32)
    tall = jnp.concatenate([image, start[...], unit], axis=1)
    _, solved = eliminate(gram, tall)
    image = solved[:, :width]
    image_out[...] = image
    for i in range(grid_rows):
        copies[i] = image
    basis[...] = solved[:, width : 2 * width]
    inverse[...] = solved[:, 2 * width :]


def second_kernel(grid, *refs):
    grid_rows, grid_cols, _ = grid
    received = refs[0]
    parts = refs[1 : 1 + grid_cols]
    first_image, basis, inverse, current, image_out, small, upper_out, sent = refs[1 + grid_cols :]
    onward, grams = summed(received, parts)
    k, width = onward.shape
    lane = lane_ids(k)
    projection = matmul_small(inverse[...], jnp.where(lane < k, grams, 0.0))
    squares = jnp.where(lane < k, pltpu.roll(grams, LANES - k, 1), 0.0)
    back = transpose_small(projection)
    gram = squares - matmul_small(back, projection)
    q1, w1 = basis[...], first_image[...]
    tall = jnp.concatenate(
        [w1 - matmul_small(back, q1), onward * UP - matmul_small(back, w1)], axis=1
    )
    upper, solved = eliminate(gram, tall)
    q2 = solved[:, :width]
    image = solved[:, width:] - matmul_small(upper, q1)
    current[...] = q2
    image_out[...] = image
    small[...] = projection
    upper_out[...] = upper
    local = inner(q2, image) + pltpu.roll(inner(image, image), k, 1)
    for i in range(sent.shape[0]):
        sent[i] = local


def last_kernel(root, received, current, image_in, small, upper_in, out, tri):
    k, width = current.shape
    grams = received[0]
    for i in range(1, received.shape[0]):
        grams = grams + received[i]
    lane = lane_ids(k)
    projection = jnp.where(lane < k, grams, 0.0)
    squares = jnp.where(lane < k, pltpu.roll(grams, LANES - k, 1), 0.0)
    back = transpose_small(projection)
    gram = squares - matmul_small(back, projection)
    image = image_in[...] - matmul_small(back, current[...])
    _, solved = eliminate(gram, image)
    out[...] = solved * root
    upper = upper_in[...]
    lower = transpose_small(upper)
    top = jnp.where(lane < k, small[...], pltpu.roll(lower, k, 1))
    bottom = jnp.where(lane < k, upper, pltpu.roll(projection, k, 1))
    tri[...] = jnp.concatenate([top, bottom], axis=0)[:, : 2 * k]


def shapes_of(*shapes):
    return [jax.ShapeDtypeStruct(shape, f32) for shape in shapes]


def per_device(start_block, blocks, block_rows, block_cols, counts):
    vectors, piece_len = start_block.shape
    stored = blocks[0, 0]
    slots, side, _ = stored.shape
    grid_rows, grid_cols = lax.axis_size("row"), lax.axis_size("col")
    piece_blocks = piece_len // side
    grid = (grid_rows, grid_cols, piece_blocks)
    devices = grid_rows * grid_cols
    index = (counts, block_rows[:, 0, :], block_cols[:, 0, :], stored)
    index_specs = [SMEM, SMEM, SMEM, ANY]
    wide = piece_len + LANES
    cost = pl.CostEstimate(
        flops=2 * slots * 2 * vectors * side * side,
        bytes_accessed=slots * side * side * 2,
        transcendentals=0,
    )

    def scratch(taken_blocks, total_blocks):
        return [
            pltpu.VMEM((taken_blocks, 2 * vectors, side), jnp.bfloat16),
            pltpu.VMEM((total_blocks + 1, vectors, side), f32),
            pltpu.VMEM((slots, side, side), jnp.bfloat16),
            pltpu.SemaphoreType.DMA((slots // GROUP,)),
        ]

    def along_col(parts):
        return [
            lax.ppermute(part, "col", [(i, (i + s) % grid_cols) for i in range(grid_cols)])
            for s, part in enumerate(parts, 1)
        ]

    def exchange(x, axes):
        return lax.all_to_all(x, axes, 0, 0, tiled=True)

    def turned(scale, pieces, others=()):
        n = len(pieces) + len(others)
        return pl.pallas_call(
            functools.partial(turned_kernel, grid, scale, bool(others)),
            out_shape=shapes_of((grid_rows, vectors, wide))[0],
            in_specs=index_specs + [VMEM] * n,
            out_specs=VMEM,
            scratch_shapes=scratch(grid_cols * piece_blocks, grid_rows * piece_blocks),
            cost_estimate=cost,
            name="turned",
        )(*index, *pieces, *others)

    def direct(scale, gathered):
        return pl.pallas_call(
            functools.partial(direct_kernel, grid, scale),
            out_shape=shapes_of(*[(vectors, piece_len)] * grid_cols),
            in_specs=index_specs + [VMEM],
            out_specs=[VMEM] * grid_cols,
            scratch_shapes=scratch(grid_rows * piece_blocks, grid_cols * piece_blocks),
            cost_estimate=cost,
            name="direct",
        )(*index, gathered)

    def small_call(kernel, name, inputs, outs):
        return pl.pallas_call(
            kernel,
            out_shape=shapes_of(*outs),
            in_specs=[VMEM] * len(inputs),
            out_specs=[VMEM] * len(outs),
            name=name,
        )(*inputs)

    piece = (vectors, piece_len)
    square = (vectors, LANES)

    gathered = exchange(jnp.broadcast_to(start_block[None], (grid_rows,) + piece), "row")
    start_row = [start_block] + along_col([start_block] * (grid_cols - 1))
    received = exchange(turned(1.0, start_row), "row")
    own, *rest = direct(1.0, gathered)
    parts = [own] + along_col(rest)
    image, copies, basis, inverse = small_call(
        functools.partial(first_kernel, grid),
        "first",
        [received, *parts, start_block],
        [piece, (grid_rows,) + piece, piece, square],
    )

    gathered = exchange(copies, "row")
    image_row = [image] + along_col([image] * (grid_cols - 1))
    received = exchange(turned(DOWN, image_row, start_row), "row")
    own, *rest = direct(DOWN, gathered)
    parts = [own] + along_col(rest)
    current, image, small, upper, local = small_call(
        functools.partial(second_kernel, grid),
        "second",
        [received, *parts, image, basis, inverse],
        [piece, piece, square, square, (devices,) + square],
    )

    sums = exchange(local, ("row", "col"))
    return small_call(
        functools.partial(last_kernel, math.sqrt(piece_len * devices)),
        "last",
        [sums, current, image, small, upper],
        [piece, (ITERS * vectors, ITERS * vectors)],
    )


def solution(mesh):
    placed = (
        P(None, ("row", "col")),
        P("row", "col", None, None, None),
        P(None, "col", None),
        P(None, "col", None),
        P(),
    )

    def step(*arrays):
        next_block, tridiagonal = jax.shard_map(
            per_device,
            mesh=mesh,
            in_specs=placed,
            out_specs=(P(None, ("row", "col")), P()),
            check_vma=False,
        )(*arrays)
        return next_block, tridiagonal

    return step
```

```python
import functools
import math

import jax
import jax.numpy as jnp
from jax import lax
from jax.experimental import pallas as pl
from jax.experimental.pallas import tpu as pltpu
from jax.sharding import PartitionSpec as P

ITERS = 2
LANES = 128
GROUP = 16
HELD = 2
DOWN = 2.0**-6
UP = 2.0**6

VMEM = pl.BlockSpec(memory_space=pltpu.VMEM)
SMEM = pl.BlockSpec(memory_space=pltpu.SMEM)
ANY = pl.BlockSpec(memory_space=pl.ANY)
f32 = jnp.float32


def split_terms(x):
    coarse = x.astype(jnp.bfloat16).astype(f32)
    return jnp.concatenate([coarse, x - coarse], axis=0).astype(jnp.bfloat16)


def lane_ids(k):
    return lax.broadcasted_iota(jnp.int32, (k, LANES), 1)


def row_ids(k, width):
    return lax.broadcasted_iota(jnp.int32, (k, width), 0)


def inner(left, right):
    k, width = left.shape
    row, lane = row_ids(k, LANES), lane_ids(k)
    result = jnp.zeros((k, LANES), f32)
    for turn in range(k):
        turned = right if turn == 0 else pltpu.roll(right, turn, 0)
        product = left * turned
        total = product[:, :LANES]
        for low in range(LANES, width, LANES):
            total = total + product[:, low : low + LANES]
        value = jnp.sum(total, axis=1, keepdims=True)
        spot = lane == jnp.where(row >= turn, row - turn, row - turn + k)
        result = jnp.where(spot, value, result)
    return result


def matmul_small(square, tall, transposed=False):
    k, width = tall.shape
    if transposed:
        square = transpose_small(square)
    result = jnp.zeros((k, width), f32)
    for i in range(k):
        result = result + square[:, i : i + 1] * tall[i : i + 1, :]
    return result


def transpose_small(square):
    k = square.shape[0]
    row, lane = row_ids(k, LANES), lane_ids(k)
    result = jnp.zeros((k, LANES), f32)
    for i in range(k):
        line = jnp.sum(
            jnp.where(lane == row_ids(k, LANES), square[:, i : i + 1], 0.0), axis=0, keepdims=True
        )
        result = jnp.where(row == i, line, result)
    return result


def eliminate(gram, tall):
    k, width = tall.shape
    row_small, row_tall = row_ids(k, LANES), row_ids(k, width)
    for i in range(k):
        column = gram[:, i : i + 1]
        scale = 1.0 / jnp.sqrt(gram[i : i + 1, i : i + 1])
        factor = column * scale
        line_small = gram[i : i + 1, :] * scale
        line_tall = tall[i : i + 1, :] * scale
        gram = jnp.where(
            row_small < i,
            gram,
            jnp.where(row_small == i, line_small, gram - factor * line_small),
        )
        tall = jnp.where(
            row_tall < i,
            tall,
            jnp.where(row_tall == i, line_tall, tall - factor * line_tall),
        )
    lane = lane_ids(k)
    upper = jnp.where((lane >= row_small) & (lane < k), gram, 0.0)
    return upper, tall


def own_place():
    return lax.axis_index("row"), lax.axis_index("col")


def opening_kernel(grid, start, blocks, block_rows, block_cols, counts, *refs):
    grid_rows, grid_cols, piece_blocks = grid
    copies, near, held, table, lines, rows_near, cols_near, counts_near, arrived = refs
    r, c = own_place()
    slots = blocks.shape[0]
    pairs = (
        (start, near),
        (block_rows, rows_near),
        (block_cols, cols_near),
        (counts, counts_near),
        (blocks.at[pl.ds(0, held.shape[0])], held),
    )
    moves = [pltpu.make_async_copy(*pair, arrived.at[i]) for i, pair in enumerate(pairs)]
    for move in moves:
        move.start()
    moves[0].wait()
    piece = near[...]
    for i in range(grid_rows):
        copies[i] = piece
    for move in moves[1:4]:
        move.wait()
    block_rows, block_cols, counts = rows_near, cols_near, counts_near
    rids, cids = block_rows[pl.ds(r, 1), :], block_cols[pl.ds(r, 1), :]
    at = (lax.broadcasted_iota(jnp.int32, counts.shape, 0) == c) & (
        lax.broadcasted_iota(jnp.int32, counts.shape, 1) == r
    )
    count = jnp.sum(
        jnp.sum(jnp.where(at, counts[...].astype(f32), 0.0), axis=1, keepdims=True),
        axis=0,
        keepdims=True,
    ).astype(jnp.int32)
    live = lax.broadcasted_iota(jnp.int32, (1, slots), 1) < count
    inside = rids - c * piece_blocks
    same = (inside == cids - r * piece_blocks) & (inside >= 0) & (inside < piece_blocks)
    lines[0:1] = rids
    lines[1:2] = cids
    lines[2:3] = jnp.where(live & jnp.logical_not(same), cids, grid_rows * piece_blocks)
    lines[3:4] = jnp.where(live, rids, grid_cols * piece_blocks)
    lines[4:5] = jnp.broadcast_to(count, (1, slots))
    listed = pltpu.make_async_copy(lines, table, arrived.at[5])
    listed.start()
    listed.wait()
    moves[4].wait()


def stream_of(count, blocks, held, streamed, arrived):
    first = held.shape[0] // GROUP
    parts = blocks.shape[0] // GROUP

    def move(part):
        rows = pl.ds((part - first) * GROUP, GROUP)
        return pltpu.make_async_copy(
            blocks.at[pl.ds(part * GROUP, GROUP)], streamed.at[rows], arrived.at[part - first]
        )

    for part in range(first, parts):

        @pl.when(part * GROUP < count)
        def _():
            move(part).start()

    def each_group(work):
        for part in range(parts):

            @pl.when(part * GROUP < count)
            def _():
                if part < first:
                    work(part * GROUP, [held.at[part * GROUP + g] for g in range(GROUP)])
                else:
                    move(part).wait()
                    low = (part - first) * GROUP
                    work(part * GROUP, [streamed.at[low + g] for g in range(GROUP)])

    return each_group


def turned_kernel(grid, scale, pairs, *refs):
    grid_rows, grid_cols, piece_blocks = grid
    table, held, blocks = refs[:3]
    pieces = refs[3 : 3 + grid_cols]
    others = refs[3 + grid_cols : 3 + 2 * grid_cols] if pairs else None
    sent, taken, total, streamed, arrived = refs[-5:]
    _, c = own_place()
    each_group = stream_of(table[4, 0], blocks, held, streamed, arrived)
    vectors = pieces[0].shape[0]
    for shift in range(grid_cols):
        place = lax.rem(c - shift + grid_cols, grid_cols) * piece_blocks
        for b in range(piece_blocks):
            x = pieces[shift][:, b * LANES : (b + 1) * LANES]
            taken[place + b] = split_terms(x * scale if scale != 1.0 else x)
    total[...] = jnp.zeros_like(total)

    def work(first, group):
        for g in range(GROUP):
            slot = first + g
            y = jnp.dot(taken[table[0, slot]], group[g][...], preferred_element_type=f32)
            total[table[2, slot]] += y[:vectors] + y[vectors:]

    each_group(work)
    gram = jnp.zeros((vectors, LANES), f32)
    for shift in range(grid_cols):
        p = pieces[shift][...]
        if pairs:
            gram = gram + inner(others[shift][...], p) + pltpu.roll(inner(p, p), vectors, 1)
        else:
            gram = gram + inner(p, p)
    for piece in range(grid_rows):
        for b in range(piece_blocks):
            sent[piece, :, b * LANES : (b + 1) * LANES] = total[piece * piece_blocks + b]
        sent[piece, :, piece_blocks * LANES :] = gram


def direct_kernel(grid, scale, *refs):
    grid_rows, grid_cols, piece_blocks = grid
    table, held, blocks, gathered = refs[:4]
    outs = refs[4 : 4 + grid_cols]
    taken, total, streamed, arrived = refs[-4:]
    _, c = own_place()
    each_group = stream_of(table[4, 0], blocks, held, streamed, arrived)
    vectors = gathered.shape[1]
    for piece in range(grid_rows):
        for b in range(piece_blocks):
            x = gathered[piece, :, b * LANES : (b + 1) * LANES]
            taken[piece * piece_blocks + b] = split_terms(x * scale if scale != 1.0 else x)
    total[...] = jnp.zeros_like(total)

    def work(first, group):
        for g in range(GROUP):
            slot = first + g
            y = lax.dot_general(
                taken[table[1, slot]],
                group[g][...],
                (((1,), (1,)), ((), ())),
                preferred_element_type=f32,
            )
            total[table[3, slot]] += y[:vectors] + y[vectors:]

    each_group(work)
    for shift in range(grid_cols):
        place = lax.rem(c + shift, grid_cols) * piece_blocks
        for b in range(piece_blocks):
            outs[shift][:, b * LANES : (b + 1) * LANES] = total[place + b]


def summed(received, parts):
    piece_len = parts[0].shape[1]
    whole = received[0]
    for i in range(1, received.shape[0]):
        whole = whole + received[i]
    image = whole[:, :piece_len]
    for part in parts:
        image = image + part[...]
    return image, whole[:, piece_len:]


def first_kernel(grid, *refs):
    grid_rows, grid_cols, _ = grid
    received = refs[0]
    parts = refs[1 : 1 + grid_cols]
    start, image_out, copies, basis, inverse = refs[1 + grid_cols :]
    image, gram = summed(received, parts)
    k, width = image.shape
    unit = (lane_ids(k) == row_ids(k, LANES)).astype(f32)
    tall = jnp.concatenate([image, start[...], unit], axis=1)
    _, solved = eliminate(gram, tall)
    image = solved[:, :width]
    image_out[...] = image
    for i in range(grid_rows):
        copies[i] = image
    basis[...] = solved[:, width : 2 * width]
    inverse[...] = solved[:, 2 * width :]


def second_kernel(grid, *refs):
    grid_rows, grid_cols, _ = grid
    received = refs[0]
    parts = refs[1 : 1 + grid_cols]
    first_image, basis, inverse, current, image_out, small, upper_out, sent = refs[1 + grid_cols :]
    onward, grams = summed(received, parts)
    k, width = onward.shape
    lane = lane_ids(k)
    projection = matmul_small(inverse[...], jnp.where(lane < k, grams, 0.0))
    squares = jnp.where(lane < k, pltpu.roll(grams, LANES - k, 1), 0.0)
    back = transpose_small(projection)
    gram = squares - matmul_small(back, projection)
    q1, w1 = basis[...], first_image[...]
    tall = jnp.concatenate(
        [w1 - matmul_small(back, q1), onward * UP - matmul_small(back, w1)], axis=1
    )
    upper, solved = eliminate(gram, tall)
    q2 = solved[:, :width]
    image = solved[:, width:] - matmul_small(upper, q1)
    current[...] = q2
    image_out[...] = image
    small[...] = projection
    upper_out[...] = upper
    local = inner(q2, image) + pltpu.roll(inner(image, image), k, 1)
    for i in range(sent.shape[0]):
        sent[i] = local


def last_kernel(root, received, current, image_in, small, upper_in, out, tri):
    k, width = current.shape
    grams = received[0]
    for i in range(1, received.shape[0]):
        grams = grams + received[i]
    lane = lane_ids(k)
    projection = jnp.where(lane < k, grams, 0.0)
    squares = jnp.where(lane < k, pltpu.roll(grams, LANES - k, 1), 0.0)
    back = transpose_small(projection)
    gram = squares - matmul_small(back, projection)
    image = image_in[...] - matmul_small(back, current[...])
    _, solved = eliminate(gram, image)
    out[...] = solved * root
    upper = upper_in[...]
    lower = transpose_small(upper)
    top = jnp.where(lane < k, small[...], pltpu.roll(lower, k, 1))
    bottom = jnp.where(lane < k, upper, pltpu.roll(projection, k, 1))
    tri[...] = jnp.concatenate([top, bottom], axis=0)[:, : 2 * k]


def shapes_of(*shapes):
    return [jax.ShapeDtypeStruct(shape, f32) for shape in shapes]


def per_device(start_block, blocks, block_rows, block_cols, counts):
    vectors, piece_len = start_block.shape
    stored = blocks[0, 0]
    slots, side, _ = stored.shape
    grid_rows, grid_cols = lax.axis_size("row"), lax.axis_size("col")
    piece_blocks = piece_len // side
    grid = (grid_rows, grid_cols, piece_blocks)
    devices = grid_rows * grid_cols
    wide = piece_len + LANES
    keep = slots // HELD
    cost = pl.CostEstimate(
        flops=2 * slots * 2 * vectors * side * side,
        bytes_accessed=slots * side * side * 2,
        transcendentals=0,
    )

    limits = pltpu.CompilerParams(vmem_limit_bytes=16 << 20)

    def scratch(taken_blocks, total_blocks):
        return [
            pltpu.VMEM((taken_blocks, 2 * vectors, side), jnp.bfloat16),
            pltpu.VMEM((total_blocks + 1, vectors, side), f32),
            pltpu.VMEM((slots - keep, side, side), jnp.bfloat16),
            pltpu.SemaphoreType.DMA(((slots - keep) // GROUP,)),
        ]

    def along_col(parts):
        return [
            lax.ppermute(part, "col", [(i, (i + s) % grid_cols) for i in range(grid_cols)])
            for s, part in enumerate(parts, 1)
        ]

    def exchange(x, axes):
        return lax.all_to_all(x, axes, 0, 0, tiled=True)

    def turned(scale, pieces, others=()):
        n = len(pieces) + len(others)
        return pl.pallas_call(
            functools.partial(turned_kernel, grid, scale, bool(others)),
            out_shape=shapes_of((grid_rows, vectors, wide))[0],
            in_specs=[SMEM, VMEM, ANY] + [VMEM] * n,
            out_specs=VMEM,
            scratch_shapes=scratch(grid_cols * piece_blocks, grid_rows * piece_blocks),
            cost_estimate=cost,
            compiler_params=limits,
            name="turned",
        )(table, held, far, *pieces, *others)

    def direct(scale, gathered):
        return pl.pallas_call(
            functools.partial(direct_kernel, grid, scale),
            out_shape=shapes_of(*[(vectors, piece_len)] * grid_cols),
            in_specs=[SMEM, VMEM, ANY] + [VMEM],
            out_specs=[VMEM] * grid_cols,
            scratch_shapes=scratch(grid_rows * piece_blocks, grid_cols * piece_blocks),
            cost_estimate=cost,
            compiler_params=limits,
            name="direct",
        )(table, held, far, gathered)

    def small_call(kernel, name, inputs, outs):
        return pl.pallas_call(
            kernel,
            out_shape=shapes_of(*outs),
            in_specs=[VMEM] * len(inputs),
            out_specs=[VMEM] * len(outs),
            compiler_params=limits,
            name=name,
        )(*inputs)

    piece = (vectors, piece_len)
    square = (vectors, LANES)

    def pinned(x):
        return pltpu.with_memory_space_constraint(x, pltpu.HBM)

    index = (block_rows[:, 0, :], block_cols[:, 0, :], counts.T)
    far = pinned(stored)
    copies, near, held, table = pl.pallas_call(
        functools.partial(opening_kernel, grid),
        out_shape=[
            shapes_of((grid_rows,) + piece)[0],
            pltpu.VMEM(piece, f32),
            pltpu.VMEM((keep, side, side), stored.dtype),
            pltpu.SMEM((8, slots), jnp.int32),
        ],
        in_specs=[ANY] * 5,
        out_specs=[VMEM, VMEM, VMEM, SMEM],
        scratch_shapes=[
            pltpu.VMEM((8, slots), jnp.int32),
            *(pltpu.VMEM(x.shape, x.dtype) for x in index),
            pltpu.SemaphoreType.DMA((6,)),
        ],
        compiler_params=limits,
        name="opening",
    )(pinned(start_block), far, *map(pinned, index))
    gathered = exchange(copies, "row")
    start_row = [near] + along_col([near] * (grid_cols - 1))
    received = exchange(turned(1.0, start_row), "row")
    own, *rest = direct(1.0, gathered)
    parts = [own] + along_col(rest)
    image, copies, basis, inverse = small_call(
        functools.partial(first_kernel, grid),
        "first",
        [received, *parts, near],
        [piece, (grid_rows,) + piece, piece, square],
    )

    gathered = exchange(copies, "row")
    image_row = [image] + along_col([image] * (grid_cols - 1))
    received = exchange(turned(DOWN, image_row, start_row), "row")
    own, *rest = direct(DOWN, gathered)
    parts = [own] + along_col(rest)
    current, image, small, upper, local = small_call(
        functools.partial(second_kernel, grid),
        "second",
        [received, *parts, image, basis, inverse],
        [piece, piece, square, square, (devices,) + square],
    )

    sums = exchange(local, ("row", "col"))
    return small_call(
        functools.partial(last_kernel, math.sqrt(piece_len * devices)),
        "last",
        [sums, current, image, small, upper],
        [piece, (ITERS * vectors, ITERS * vectors)],
    )


def solution(mesh):
    placed = (
        P(None, ("row", "col")),
        P("row", "col", None, None, None),
        P(None, "col", None),
        P(None, "col", None),
        P(),
    )

    def step(*arrays):
        next_block, tridiagonal = jax.shard_map(
            per_device,
            mesh=mesh,
            in_specs=placed,
            out_specs=(P(None, ("row", "col")), P()),
            check_vma=False,
        )(*arrays)
        return next_block, tridiagonal

    return step
```

```python
import functools
import math

import jax
import jax.numpy as jnp
from jax import lax
from jax.experimental import pallas as pl
from jax.experimental.pallas import tpu as pltpu
from jax.sharding import PartitionSpec as P

ITERS = 2
LANES = 128
GROUP = 32
HELD = 2
DOWN = 2.0**-6
UP = 2.0**6

VMEM = pl.BlockSpec(memory_space=pltpu.VMEM)
SMEM = pl.BlockSpec(memory_space=pltpu.SMEM)
ANY = pl.BlockSpec(memory_space=pl.ANY)
f32 = jnp.float32


def split_terms(x):
    coarse = x.astype(jnp.bfloat16).astype(f32)
    return jnp.concatenate([coarse, x - coarse], axis=0).astype(jnp.bfloat16)


def lane_ids(k):
    return lax.broadcasted_iota(jnp.int32, (k, LANES), 1)


def row_ids(k, width):
    return lax.broadcasted_iota(jnp.int32, (k, width), 0)


def inner(left, right):
    k, width = left.shape
    row, lane = row_ids(k, LANES), lane_ids(k)
    result = jnp.zeros((k, LANES), f32)
    for turn in range(k):
        turned = right if turn == 0 else pltpu.roll(right, turn, 0)
        product = left * turned
        total = product[:, :LANES]
        for low in range(LANES, width, LANES):
            total = total + product[:, low : low + LANES]
        value = jnp.sum(total, axis=1, keepdims=True)
        spot = lane == jnp.where(row >= turn, row - turn, row - turn + k)
        result = jnp.where(spot, value, result)
    return result


def matmul_small(square, tall, transposed=False):
    k, width = tall.shape
    if transposed:
        square = transpose_small(square)
    result = jnp.zeros((k, width), f32)
    for i in range(k):
        result = result + square[:, i : i + 1] * tall[i : i + 1, :]
    return result


def transpose_small(square):
    k = square.shape[0]
    row, lane = row_ids(k, LANES), lane_ids(k)
    result = jnp.zeros((k, LANES), f32)
    for i in range(k):
        line = jnp.sum(
            jnp.where(lane == row_ids(k, LANES), square[:, i : i + 1], 0.0), axis=0, keepdims=True
        )
        result = jnp.where(row == i, line, result)
    return result


def eliminate(gram, tall):
    k, width = tall.shape
    row_small, row_tall = row_ids(k, LANES), row_ids(k, width)
    for i in range(k):
        column = gram[:, i : i + 1]
        scale = 1.0 / jnp.sqrt(gram[i : i + 1, i : i + 1])
        factor = column * scale
        line_small = gram[i : i + 1, :] * scale
        line_tall = tall[i : i + 1, :] * scale
        gram = jnp.where(
            row_small < i,
            gram,
            jnp.where(row_small == i, line_small, gram - factor * line_small),
        )
        tall = jnp.where(
            row_tall < i,
            tall,
            jnp.where(row_tall == i, line_tall, tall - factor * line_tall),
        )
    lane = lane_ids(k)
    upper = jnp.where((lane >= row_small) & (lane < k), gram, 0.0)
    return upper, tall


def own_place():
    return lax.axis_index("row"), lax.axis_index("col")


def opening_kernel(grid, start, blocks, block_rows, block_cols, counts, *refs):
    grid_rows, grid_cols, piece_blocks = grid
    copies, near, held, table, lines, rows_near, cols_near, counts_near, arrived, left = refs
    r, c = own_place()
    slots = blocks.shape[0]
    pairs = (
        (start, near),
        (block_rows, rows_near),
        (block_cols, cols_near),
        (counts, counts_near),
        (blocks.at[pl.ds(0, held.shape[0])], held),
    )
    moves = [pltpu.make_async_copy(*pair, arrived.at[i]) for i, pair in enumerate(pairs)]
    for move in moves:
        move.start()
    moves[0].wait()
    spread = [pltpu.make_async_copy(near, copies.at[i], left.at[i]) for i in range(grid_rows)]
    for move in spread:
        move.start()
    for move in moves[1:4]:
        move.wait()
    block_rows, block_cols, counts = rows_near, cols_near, counts_near
    rids, cids = block_rows[pl.ds(r, 1), :], block_cols[pl.ds(r, 1), :]
    at = (lax.broadcasted_iota(jnp.int32, counts.shape, 0) == c) & (
        lax.broadcasted_iota(jnp.int32, counts.shape, 1) == r
    )
    count = jnp.sum(
        jnp.sum(jnp.where(at, counts[...].astype(f32), 0.0), axis=1, keepdims=True),
        axis=0,
        keepdims=True,
    ).astype(jnp.int32)
    live = lax.broadcasted_iota(jnp.int32, (1, slots), 1) < count
    inside = rids - c * piece_blocks
    same = (inside == cids - r * piece_blocks) & (inside >= 0) & (inside < piece_blocks)
    lines[0:1] = rids
    lines[1:2] = cids
    tile = cids
    for piece in range(1, grid_rows):
        tile = tile + (cids >= piece * piece_blocks).astype(jnp.int32)
    lines[2:3] = jnp.where(live & jnp.logical_not(same), tile, piece_blocks)
    lines[3:4] = jnp.where(live, rids, grid_cols * piece_blocks)
    lines[4:5] = jnp.broadcast_to(count, (1, slots))
    listed = pltpu.make_async_copy(lines, table, arrived.at[5])
    listed.start()
    listed.wait()
    for move in [moves[4], *spread]:
        move.wait()


def stream_of(count, blocks, held, streamed, arrived):
    first = held.shape[0] // GROUP
    parts = blocks.shape[0] // GROUP

    def move(part):
        rows = pl.ds((part - first) * GROUP, GROUP)
        return pltpu.make_async_copy(
            blocks.at[pl.ds(part * GROUP, GROUP)], streamed.at[rows], arrived.at[part - first]
        )

    for part in range(first, parts):

        @pl.when(part * GROUP < count)
        def _():
            move(part).start()

    def each_group(work):
        for part in range(parts):

            @pl.when(part * GROUP < count)
            def _():
                if part < first:
                    work(part * GROUP, [held.at[part * GROUP + g] for g in range(GROUP)])
                else:
                    move(part).wait()
                    low = (part - first) * GROUP
                    work(part * GROUP, [streamed.at[low + g] for g in range(GROUP)])

    return each_group


def store_pair(total, one, two, y):
    k = y.shape[0] // 4
    side = y.shape[1] // 2
    total[one] += y[:k, :side] + y[k : 2 * k, :side]
    total[two] += y[2 * k : 3 * k, side:] + y[3 * k :, side:]


def turned_kernel(grid, scale, pairs, *refs):
    grid_rows, grid_cols, piece_blocks = grid
    table, held, blocks = refs[:3]
    pieces = refs[3 : 3 + grid_cols]
    others = refs[3 + grid_cols : 3 + 2 * grid_cols] if pairs else None
    sent, taken, streamed, arrived = refs[-4:]
    _, c = own_place()
    each_group = stream_of(table[4, 0], blocks, held, streamed, arrived)
    vectors = pieces[0].shape[0]
    for shift in range(grid_cols):
        place = lax.rem(c - shift + grid_cols, grid_cols) * piece_blocks
        for b in range(piece_blocks):
            x = pieces[shift][:, b * LANES : (b + 1) * LANES]
            taken[place + b] = split_terms(x * scale if scale != 1.0 else x)
    sent[...] = jnp.zeros_like(sent)

    def work(first, group):
        for g in range(0, GROUP, 2):
            one, two = first + g, first + g + 1
            y = jnp.dot(
                jnp.concatenate([taken[table[0, one]], taken[table[0, two]]], axis=0),
                jnp.concatenate([group[g][...], group[g + 1][...]], axis=1),
                preferred_element_type=f32,
            )
            store_pair(sent, table[2, one], table[2, two], y)

    each_group(work)
    gram = jnp.zeros((vectors, LANES), f32)
    for shift in range(grid_cols):
        p = pieces[shift][...]
        if pairs:
            gram = gram + inner(others[shift][...], p) + pltpu.roll(inner(p, p), vectors, 1)
        else:
            gram = gram + inner(p, p)
    for piece in range(grid_rows):
        sent[piece * (piece_blocks + 1) + piece_blocks] = gram


def direct_kernel(grid, scale, *refs):
    grid_rows, grid_cols, piece_blocks = grid
    table, held, blocks, gathered = refs[:4]
    outs = refs[4 : 4 + grid_cols]
    taken, total, streamed, arrived = refs[-4:]
    _, c = own_place()
    each_group = stream_of(table[4, 0], blocks, held, streamed, arrived)
    vectors = gathered.shape[1]
    for piece in range(grid_rows):
        for b in range(piece_blocks):
            x = gathered[piece, :, b * LANES : (b + 1) * LANES]
            taken[piece * piece_blocks + b] = split_terms(x * scale if scale != 1.0 else x)
    total[...] = jnp.zeros_like(total)

    def work(first, group):
        for g in range(0, GROUP, 2):
            one, two = first + g, first + g + 1
            y = lax.dot_general(
                jnp.concatenate([taken[table[1, one]], taken[table[1, two]]], axis=0),
                jnp.concatenate([group[g][...], group[g + 1][...]], axis=0),
                (((1,), (1,)), ((), ())),
                preferred_element_type=f32,
            )
            store_pair(total, table[3, one], table[3, two], y)

    each_group(work)
    for shift in range(grid_cols):
        place = lax.rem(c + shift, grid_cols) * piece_blocks
        for b in range(piece_blocks):
            outs[shift][:, b * LANES : (b + 1) * LANES] = total[place + b]


def summed(received, parts):
    tiles = parts[0].shape[1] // LANES + 1
    sums = []
    for b in range(tiles):
        whole = received[b]
        for i in range(b + tiles, received.shape[0], tiles):
            whole = whole + received[i]
        sums.append(whole)
    image = jnp.concatenate(sums[:-1], axis=1)
    for part in parts:
        image = image + part[...]
    return image, sums[-1]


def first_kernel(grid, *refs):
    grid_rows, grid_cols, _ = grid
    received = refs[0]
    parts = refs[1 : 1 + grid_cols]
    start, image_out, copies, basis, inverse = refs[1 + grid_cols :]
    image, gram = summed(received, parts)
    k, width = image.shape
    unit = (lane_ids(k) == row_ids(k, LANES)).astype(f32)
    tall = jnp.concatenate([image, start[...], unit], axis=1)
    _, solved = eliminate(gram, tall)
    image = solved[:, :width]
    image_out[...] = image
    for i in range(grid_rows):
        copies[i] = image
    basis[...] = solved[:, width : 2 * width]
    inverse[...] = solved[:, 2 * width :]


def second_kernel(grid, *refs):
    grid_rows, grid_cols, _ = grid
    received = refs[0]
    parts = refs[1 : 1 + grid_cols]
    first_image, basis, inverse, current, image_out, small, upper_out, sent = refs[1 + grid_cols :]
    onward, grams = summed(received, parts)
    k, width = onward.shape
    lane = lane_ids(k)
    projection = matmul_small(inverse[...], jnp.where(lane < k, grams, 0.0))
    squares = jnp.where(lane < k, pltpu.roll(grams, LANES - k, 1), 0.0)
    back = transpose_small(projection)
    gram = squares - matmul_small(back, projection)
    q1, w1 = basis[...], first_image[...]
    tall = jnp.concatenate(
        [w1 - matmul_small(back, q1), onward * UP - matmul_small(back, w1)], axis=1
    )
    upper, solved = eliminate(gram, tall)
    q2 = solved[:, :width]
    image = solved[:, width:] - matmul_small(upper, q1)
    current[...] = q2
    image_out[...] = image
    small[...] = projection
    upper_out[...] = upper
    local = inner(q2, image) + pltpu.roll(inner(image, image), k, 1)
    line = local[:1]
    for i in range(1, k):
        line = line + pltpu.roll(local[i : i + 1], 2 * k * i, 1)
    sent[...] = jnp.broadcast_to(line[None], sent.shape)


def last_kernel(root, received, current, image_in, small, upper_in, out, tri):
    k, width = current.shape
    line = jnp.sum(received[...], axis=0)
    lane = lane_ids(k)
    grams = jnp.concatenate(
        [line] + [pltpu.roll(line, LANES - 2 * k * i, 1) for i in range(1, k)], axis=0
    )
    projection = jnp.where(lane < k, grams, 0.0)
    squares = jnp.where(lane < k, pltpu.roll(grams, LANES - k, 1), 0.0)
    back = transpose_small(projection)
    gram = squares - matmul_small(back, projection)
    image = image_in[...] - matmul_small(back, current[...])
    _, solved = eliminate(gram, image)
    out[...] = solved * root
    upper = upper_in[...]
    lower = transpose_small(upper)
    top = jnp.where(lane < k, small[...], pltpu.roll(lower, k, 1))
    bottom = jnp.where(lane < k, upper, pltpu.roll(projection, k, 1))
    tri[...] = jnp.concatenate([top, bottom], axis=0)[:, : 2 * k]


def shapes_of(*shapes):
    return [jax.ShapeDtypeStruct(shape, f32) for shape in shapes]


def per_device(start_block, blocks, block_rows, block_cols, counts):
    vectors, piece_len = start_block.shape
    stored = blocks[0, 0]
    slots, side, _ = stored.shape
    grid_rows, grid_cols = lax.axis_size("row"), lax.axis_size("col")
    piece_blocks = piece_len // side
    grid = (grid_rows, grid_cols, piece_blocks)
    devices = grid_rows * grid_cols
    keep = slots // HELD
    cost = pl.CostEstimate(
        flops=2 * slots * 2 * vectors * side * side,
        bytes_accessed=slots * side * side * 2,
        transcendentals=0,
    )

    limits = pltpu.CompilerParams(vmem_limit_bytes=16 << 20)

    def scratch(taken_blocks, *total):
        return [
            pltpu.VMEM((taken_blocks, 2 * vectors, side), jnp.bfloat16),
            *total,
            pltpu.VMEM((slots - keep, side, side), jnp.bfloat16),
            pltpu.SemaphoreType.DMA(((slots - keep) // GROUP,)),
        ]

    def along_col(parts):
        return [
            lax.ppermute(part, "col", [(i, (i + s) % grid_cols) for i in range(grid_cols)])
            for s, part in enumerate(parts, 1)
        ]

    def exchange(x, axes):
        return lax.all_to_all(x, axes, 0, 0, tiled=True)

    def turned(scale, pieces, others=()):
        n = len(pieces) + len(others)
        return pl.pallas_call(
            functools.partial(turned_kernel, grid, scale, bool(others)),
            out_shape=shapes_of((grid_rows * (piece_blocks + 1), vectors, side))[0],
            in_specs=[SMEM, VMEM, ANY] + [VMEM] * n,
            out_specs=VMEM,
            scratch_shapes=scratch(grid_cols * piece_blocks),
            cost_estimate=cost,
            compiler_params=limits,
            name="turned",
        )(table, held, far, *pieces, *others)

    def direct(scale, gathered):
        return pl.pallas_call(
            functools.partial(direct_kernel, grid, scale),
            out_shape=shapes_of(*[(vectors, piece_len)] * grid_cols),
            in_specs=[SMEM, VMEM, ANY] + [VMEM],
            out_specs=[VMEM] * grid_cols,
            scratch_shapes=scratch(
                grid_rows * piece_blocks,
                pltpu.VMEM((grid_cols * piece_blocks + 1, vectors, side), f32),
            ),
            cost_estimate=cost,
            compiler_params=limits,
            name="direct",
        )(table, held, far, gathered)

    def small_call(kernel, name, inputs, outs):
        return pl.pallas_call(
            kernel,
            out_shape=shapes_of(*outs),
            in_specs=[VMEM] * len(inputs),
            out_specs=[VMEM] * len(outs),
            compiler_params=limits,
            name=name,
        )(*inputs)

    piece = (vectors, piece_len)
    square = (vectors, LANES)

    def pinned(x):
        return pltpu.with_memory_space_constraint(x, pltpu.HBM)

    index = (block_rows[:, 0, :], block_cols[:, 0, :], counts.T)
    far = pinned(stored)
    copies, near, held, table = pl.pallas_call(
        functools.partial(opening_kernel, grid),
        out_shape=[
            shapes_of((grid_rows,) + piece)[0],
            pltpu.VMEM(piece, f32),
            pltpu.VMEM((keep, side, side), stored.dtype),
            pltpu.SMEM((8, slots), jnp.int32),
        ],
        in_specs=[ANY] * 5,
        out_specs=[ANY, VMEM, VMEM, SMEM],
        scratch_shapes=[
            pltpu.VMEM((8, slots), jnp.int32),
            *(pltpu.VMEM(x.shape, x.dtype) for x in index),
            pltpu.SemaphoreType.DMA((6,)),
            pltpu.SemaphoreType.DMA((grid_rows,)),
        ],
        compiler_params=limits,
        name="opening",
    )(pinned(start_block), far, *map(pinned, index))
    gathered = exchange(copies, "row")
    start_row = [near] + along_col([near] * (grid_cols - 1))
    received = exchange(turned(1.0, start_row), "row")
    own, *rest = direct(1.0, gathered)
    parts = [own] + along_col(rest)
    image, copies, basis, inverse = small_call(
        functools.partial(first_kernel, grid),
        "first",
        [received, *parts, near],
        [piece, (grid_rows,) + piece, piece, square],
    )

    gathered = exchange(copies, "row")
    image_row = [image] + along_col([image] * (grid_cols - 1))
    received = exchange(turned(DOWN, image_row, start_row), "row")
    own, *rest = direct(DOWN, gathered)
    parts = [own] + along_col(rest)
    current, image, small, upper, local = small_call(
        functools.partial(second_kernel, grid),
        "second",
        [received, *parts, image, basis, inverse],
        [piece, piece, square, square, (devices, 1, LANES)],
    )

    sums = exchange(local, ("row", "col"))
    return small_call(
        functools.partial(last_kernel, math.sqrt(piece_len * devices)),
        "last",
        [sums, current, image, small, upper],
        [piece, (ITERS * vectors, ITERS * vectors)],
    )


def solution(mesh):
    placed = (
        P(None, ("row", "col")),
        P("row", "col", None, None, None),
        P(None, "col", None),
        P(None, "col", None),
        P(),
    )

    def step(*arrays):
        next_block, tridiagonal = jax.shard_map(
            per_device,
            mesh=mesh,
            in_specs=placed,
            out_specs=(P(None, ("row", "col")), P()),
            check_vma=False,
        )(*arrays)
        return next_block, tridiagonal

    return step
```

```python
import functools
import math

import jax
import jax.numpy as jnp
from jax import lax
from jax.experimental import pallas as pl
from jax.experimental.pallas import tpu as pltpu
from jax.sharding import PartitionSpec as P

ITERS = 2
LANES = 128
GROUP = 32
HELD = 2
DOWN = 2.0**-2
LOW = 2.0**-4

VMEM = pl.BlockSpec(memory_space=pltpu.VMEM)
SMEM = pl.BlockSpec(memory_space=pltpu.SMEM)
ANY = pl.BlockSpec(memory_space=pl.ANY)
f32 = jnp.float32


def split_terms(x):
    coarse = x.astype(jnp.bfloat16).astype(f32)
    return jnp.concatenate([coarse, x - coarse], axis=0).astype(jnp.bfloat16)


def lane_ids(k):
    return lax.broadcasted_iota(jnp.int32, (k, LANES), 1)


def row_ids(k, width):
    return lax.broadcasted_iota(jnp.int32, (k, width), 0)


def inner(left, right):
    k, width = left.shape
    row, lane = row_ids(k, LANES), lane_ids(k)
    result = jnp.zeros((k, LANES), f32)
    for turn in range(k):
        turned = right if turn == 0 else pltpu.roll(right, turn, 0)
        product = left * turned
        total = product[:, :LANES]
        for low in range(LANES, width, LANES):
            total = total + product[:, low : low + LANES]
        value = jnp.sum(total, axis=1, keepdims=True)
        spot = lane == jnp.where(row >= turn, row - turn, row - turn + k)
        result = jnp.where(spot, value, result)
    return result


def matmul_small(square, tall, transposed=False):
    k, width = tall.shape
    if transposed:
        square = transpose_small(square)
    result = jnp.zeros((k, width), f32)
    for i in range(k):
        result = result + square[:, i : i + 1] * tall[i : i + 1, :]
    return result


def transpose_small(square):
    k = square.shape[0]
    row, lane = row_ids(k, LANES), lane_ids(k)
    result = jnp.zeros((k, LANES), f32)
    for i in range(k):
        line = jnp.sum(
            jnp.where(lane == row_ids(k, LANES), square[:, i : i + 1], 0.0), axis=0, keepdims=True
        )
        result = jnp.where(row == i, line, result)
    return result


def eliminate(gram, tall):
    k, width = tall.shape
    row_small, row_tall = row_ids(k, LANES), row_ids(k, width)
    for i in range(k):
        column = gram[:, i : i + 1]
        scale = 1.0 / jnp.sqrt(gram[i : i + 1, i : i + 1])
        factor = column * scale
        line_small = gram[i : i + 1, :] * scale
        line_tall = tall[i : i + 1, :] * scale
        gram = jnp.where(
            row_small < i,
            gram,
            jnp.where(row_small == i, line_small, gram - factor * line_small),
        )
        tall = jnp.where(
            row_tall < i,
            tall,
            jnp.where(row_tall == i, line_tall, tall - factor * line_tall),
        )
    lane = lane_ids(k)
    upper = jnp.where((lane >= row_small) & (lane < k), gram, 0.0)
    return upper, tall


def own_place():
    return lax.axis_index("row"), lax.axis_index("col")


def opening_kernel(grid, start, blocks, block_rows, block_cols, counts, *refs):
    grid_rows, grid_cols, piece_blocks = grid
    near, held, table, lines, rows_near, cols_near, counts_near, arrived = refs
    r, c = own_place()
    slots = blocks.shape[0]
    pairs = (
        (start, near),
        (block_rows, rows_near),
        (block_cols, cols_near),
        (counts, counts_near),
        (blocks.at[pl.ds(0, held.shape[0])], held),
    )
    moves = [pltpu.make_async_copy(*pair, arrived.at[i]) for i, pair in enumerate(pairs)]
    for move in moves:
        move.start()
    for move in moves[1:4]:
        move.wait()
    block_rows, block_cols, counts = rows_near, cols_near, counts_near
    rids, cids = block_rows[pl.ds(r, 1), :], block_cols[pl.ds(r, 1), :]
    at = (lax.broadcasted_iota(jnp.int32, counts.shape, 0) == c) & (
        lax.broadcasted_iota(jnp.int32, counts.shape, 1) == r
    )
    count = jnp.sum(
        jnp.sum(jnp.where(at, counts[...].astype(f32), 0.0), axis=1, keepdims=True),
        axis=0,
        keepdims=True,
    ).astype(jnp.int32)
    live = lax.broadcasted_iota(jnp.int32, (1, slots), 1) < count
    inside = rids - c * piece_blocks
    same = (inside == cids - r * piece_blocks) & (inside >= 0) & (inside < piece_blocks)
    lines[0:1] = rids
    lines[1:2] = cids
    tile = cids
    for piece in range(1, grid_rows):
        tile = tile + (cids >= piece * piece_blocks).astype(jnp.int32)
    lines[2:3] = jnp.where(live & jnp.logical_not(same), tile, piece_blocks)
    lines[3:4] = jnp.where(live, rids, grid_cols * piece_blocks)
    lines[4:5] = jnp.broadcast_to(count, (1, slots))
    listed = pltpu.make_async_copy(lines, table, arrived.at[5])
    listed.start()
    listed.wait()
    moves[0].wait()
    moves[4].wait()


def stream_of(count, blocks, held, streamed, arrived):
    first = held.shape[0] // GROUP
    parts = blocks.shape[0] // GROUP

    def move(part):
        rows = pl.ds((part - first) * GROUP, GROUP)
        return pltpu.make_async_copy(
            blocks.at[pl.ds(part * GROUP, GROUP)], streamed.at[rows], arrived.at[part - first]
        )

    for part in range(first, parts):

        @pl.when(part * GROUP < count)
        def _():
            move(part).start()

    def each_group(work):
        for part in range(parts):

            @pl.when(part * GROUP < count)
            def _():
                if part < first:
                    work(part * GROUP, [held.at[part * GROUP + g] for g in range(GROUP)])
                else:
                    move(part).wait()
                    low = (part - first) * GROUP
                    work(part * GROUP, [streamed.at[low + g] for g in range(GROUP)])

    return each_group


def store_pair(total, one, two, y):
    k = y.shape[0] // 4
    side = y.shape[1] // 2
    total[one] += y[:k, :side] + y[k : 2 * k, :side]
    total[two] += y[2 * k : 3 * k, side:] + y[3 * k :, side:]


def turned_products(table, taken, sent, each_group):
    def work(first, group):
        for g in range(0, GROUP, 2):
            one, two = first + g, first + g + 1
            y = jnp.dot(
                jnp.concatenate([taken[table[0, one]], taken[table[0, two]]], axis=0),
                jnp.concatenate([group[g][...], group[g + 1][...]], axis=1),
                preferred_element_type=f32,
            )
            store_pair(sent, table[2, one], table[2, two], y)

    each_group(work)


def finish_sent(grid, r, sent, own, gram):
    grid_rows, _, piece_blocks = grid
    for piece in range(grid_rows):
        low = piece * (piece_blocks + 1)

        @pl.when(piece > r)
        def _():
            for b in range(piece_blocks):
                sent[low + b] = own[:, b * LANES : (b + 1) * LANES]

        sent[low + piece_blocks] = gram


def turned_first(grid, *refs):
    _, grid_cols, piece_blocks = grid
    table, held, blocks = refs[:3]
    pieces = refs[3 : 3 + grid_cols]
    sent, taken, streamed, arrived = refs[-4:]
    r, c = own_place()
    each_group = stream_of(table[4, 0], blocks, held, streamed, arrived)
    sent[...] = jnp.zeros_like(sent)
    gram = jnp.zeros(sent.shape[1:], f32)
    for shift in range(grid_cols):
        place = lax.rem(c - shift + grid_cols, grid_cols) * piece_blocks
        p = pieces[shift][...]
        for b in range(piece_blocks):
            taken[place + b] = split_terms(p[:, b * LANES : (b + 1) * LANES])
        gram = gram + inner(p, p)
    turned_products(table, taken, sent, each_group)
    finish_sent(grid, r, sent, pieces[0][...], gram)


def norms_of(gram):
    k = gram.shape[0]
    squares = jnp.sum(jnp.where(lane_ids(k) == row_ids(k, LANES), gram, 0.0), axis=1, keepdims=True)
    return 1.0 / jnp.sqrt(squares)


def turned_second(grid, *refs):
    _, grid_cols, piece_blocks = grid
    table, held, blocks, mine, theirs, start_gram = refs[:6]
    pieces = refs[6 : 6 + grid_cols]
    sent, low_out, taken, streamed, arrived = refs[-5:]
    r, c = own_place()
    each_group = stream_of(table[4, 0], blocks, held, streamed, arrived)
    sent[...] = jnp.zeros_like(sent)
    norms = norms_of(start_gram[...])
    factor = jnp.broadcast_to(norms * DOWN, sent.shape[1:])
    cross = jnp.zeros(sent.shape[1:], f32)
    square = jnp.zeros(sent.shape[1:], f32)
    for shift in range(grid_cols):
        place = lax.rem(c - shift + grid_cols, grid_cols) * piece_blocks
        tiles = [(mine[place + b] + theirs[place + b]) * factor for b in range(piece_blocks)]
        for b in range(piece_blocks):
            taken[place + b] = split_terms(tiles[b] * LOW)
        p = jnp.concatenate(tiles, axis=1)
        cross = cross + inner(pieces[shift][...], p)
        square = square + inner(p, p)
        if shift == 0:
            low_out[...] = p * LOW
    turned_products(table, taken, sent, each_group)
    gram = cross * norms + pltpu.roll(square, square.shape[0], 1)
    finish_sent(grid, r, sent, low_out[...], gram)


def direct_products(grid, refs_in, total, taken, streamed, arrived):
    grid_rows, _, piece_blocks = grid
    table, held, blocks, received, own = refs_in
    r, _ = own_place()
    each_group = stream_of(table[4, 0], blocks, held, streamed, arrived)
    tiles = piece_blocks + 1
    for b in range(piece_blocks):
        mine = own[:, b * LANES : (b + 1) * LANES]
        for piece in range(grid_rows):
            x = jnp.where(piece == r, mine, received[piece * tiles + b])
            taken[piece * piece_blocks + b] = split_terms(x)
    total[...] = jnp.zeros_like(total)

    def work(first, group):
        for g in range(0, GROUP, 2):
            one, two = first + g, first + g + 1
            y = lax.dot_general(
                jnp.concatenate([taken[table[1, one]], taken[table[1, two]]], axis=0),
                jnp.concatenate([group[g][...], group[g + 1][...]], axis=0),
                (((1,), (1,)), ((), ())),
                preferred_element_type=f32,
            )
            store_pair(total, table[3, one], table[3, two], y)

    each_group(work)
    part = []
    for b in range(piece_blocks):
        whole = jnp.zeros(total.shape[1:], f32)
        for piece in range(grid_rows):
            whole = whole + jnp.where(piece >= r, received[piece * tiles + b], 0.0)
        part.append(whole)
    grams = received[piece_blocks]
    for piece in range(1, grid_rows):
        grams = grams + received[piece * tiles + piece_blocks]
    return part, grams


def direct_first(grid, *refs):
    _, _, piece_blocks = grid
    out, gram_out, taken, total, streamed, arrived = refs[-6:]
    _, c = own_place()
    part, gram = direct_products(grid, refs[:5], total, taken, streamed, arrived)
    for b in range(piece_blocks):
        total[c * piece_blocks + b] += part[b]
    out[...] = total[: out.shape[0]]
    gram_out[...] = gram


def direct_second(grid, *refs):
    _, grid_cols, piece_blocks = grid
    outs = refs[5 : 5 + grid_cols]
    gram_out, taken, total, streamed, arrived = refs[-5:]
    _, c = own_place()
    part, gram = direct_products(grid, refs[:5], total, taken, streamed, arrived)
    for shift in range(grid_cols):
        place = lax.rem(c + shift, grid_cols) * piece_blocks
        for b in range(piece_blocks):
            tile = total[place + b]
            outs[shift][:, b * LANES : (b + 1) * LANES] = tile + part[b] if shift == 0 else tile
    gram_out[...] = gram


def basis_kernel(start_gram, start, low, basis, image, inverse):
    gram = start_gram[...]
    k, width = start.shape
    same = lane_ids(k) == row_ids(k, LANES)
    norms = norms_of(gram)
    across = jnp.sum(jnp.where(same, norms, 0.0), axis=0, keepdims=True)
    tall = jnp.concatenate(
        [start[...] * norms, low[...] * (1.0 / (DOWN * LOW)), same.astype(f32)], axis=1
    )
    _, solved = eliminate(gram * norms * across, tall)
    basis[...] = solved[:, :width]
    image[...] = solved[:, width : 2 * width]
    inverse[...] = solved[:, 2 * width :]


def middle_kernel(grams_in, basis, image, inverse, current, rest, factor, small, upper_out):
    k, width = basis.shape
    lane = lane_ids(k)
    first = inverse[...]
    halves = matmul_small(first, grams_in[...])
    cross = jnp.where(lane < k, halves, 0.0)
    square = jnp.where(lane < k, pltpu.roll(halves, LANES - k, 1), 0.0)
    back = matmul_small(first, transpose_small(cross)) * (1.0 / DOWN)
    squares = matmul_small(first, transpose_small(square)) * (1.0 / DOWN**2)
    projection = transpose_small(back)
    gram = squares - matmul_small(back, projection)
    q1, w1 = basis[...], image[...]
    tall = jnp.concatenate(
        [
            w1 - matmul_small(back, q1),
            matmul_small(back * (DOWN * LOW), w1),
            first,
        ],
        axis=1,
    )
    upper, solved = eliminate(gram, tall)
    current[...] = solved[:, :width]
    rest[...] = -(solved[:, width : 2 * width] * (1.0 / (DOWN * LOW))) - matmul_small(upper, q1)
    factor[...] = solved[:, 2 * width :]
    small[...] = projection
    upper_out[...] = upper


def second_kernel(grid, *refs):
    parts = refs[: grid[1]]
    current, rest, factor, image_out, sent = refs[grid[1] :]
    onward = parts[0][...]
    for part in parts[1:]:
        onward = onward + part[...]
    k = onward.shape[0]
    image = matmul_small(factor[...], onward) * (1.0 / (DOWN * LOW)) + rest[...]
    image_out[...] = image
    local = inner(current[...], image) + pltpu.roll(inner(image, image), k, 1)
    line = local[:1]
    for i in range(1, k):
        line = line + pltpu.roll(local[i : i + 1], 2 * k * i, 1)
    sent[...] = jnp.broadcast_to(line[None], sent.shape)


def last_kernel(root, received, current, image_in, small, upper_in, out, tri):
    k, width = current.shape
    line = jnp.sum(received[...], axis=0)
    lane = lane_ids(k)
    grams = jnp.concatenate(
        [line] + [pltpu.roll(line, LANES - 2 * k * i, 1) for i in range(1, k)], axis=0
    )
    projection = jnp.where(lane < k, grams, 0.0)
    squares = jnp.where(lane < k, pltpu.roll(grams, LANES - k, 1), 0.0)
    back = transpose_small(projection)
    gram = squares - matmul_small(back, projection)
    image = image_in[...] - matmul_small(back, current[...])
    _, solved = eliminate(gram, image)
    out[...] = solved * root
    upper = upper_in[...]
    lower = transpose_small(upper)
    top = jnp.where(lane < k, small[...], pltpu.roll(lower, k, 1))
    bottom = jnp.where(lane < k, upper, pltpu.roll(projection, k, 1))
    tri[...] = jnp.concatenate([top, bottom], axis=0)[:, : 2 * k]


def shapes_of(*shapes):
    return [jax.ShapeDtypeStruct(shape, f32) for shape in shapes]


def per_device(start_block, blocks, block_rows, block_cols, counts):
    vectors, piece_len = start_block.shape
    stored = blocks[0, 0]
    slots, side, _ = stored.shape
    grid_rows, grid_cols = lax.axis_size("row"), lax.axis_size("col")
    piece_blocks = piece_len // side
    grid = (grid_rows, grid_cols, piece_blocks)
    devices = grid_rows * grid_cols
    keep = slots // HELD
    piece = (vectors, piece_len)
    square = (vectors, LANES)
    chunks = (grid_rows * (piece_blocks + 1), vectors, side)
    segment = (grid_cols * piece_blocks, vectors, side)
    cost = pl.CostEstimate(
        flops=2 * slots * 2 * vectors * side * side,
        bytes_accessed=slots * side * side * 2,
        transcendentals=0,
    )
    limits = pltpu.CompilerParams(vmem_limit_bytes=16 << 20)

    def call(kernel, name, inputs, outs, specs=None, scratch=(), cost=None):
        return pl.pallas_call(
            kernel,
            out_shape=shapes_of(*outs),
            in_specs=(specs or []) + [VMEM] * (len(inputs) - len(specs or [])),
            out_specs=[VMEM] * len(outs),
            scratch_shapes=list(scratch),
            compiler_params=limits,
            cost_estimate=cost,
            name=name,
        )(*inputs)

    def product(kernel, name, inputs, outs, taken_blocks, *total):
        scratch = [
            pltpu.VMEM((taken_blocks, 2 * vectors, side), jnp.bfloat16),
            *total,
            pltpu.VMEM((slots - keep, side, side), jnp.bfloat16),
            pltpu.SemaphoreType.DMA(((slots - keep) // GROUP,)),
        ]
        return call(
            functools.partial(kernel, grid),
            name,
            [table, held, far, *inputs],
            outs,
            [SMEM, VMEM, ANY],
            scratch,
            cost,
        )

    def along_col(parts):
        return [
            lax.ppermute(part, "col", [(i, (i + s) % grid_cols) for i in range(grid_cols)])
            for s, part in enumerate(parts, 1)
        ]

    def exchange(x, axes):
        return lax.all_to_all(x, axes, 0, 0, tiled=True)

    def pinned(x):
        return pltpu.with_memory_space_constraint(x, pltpu.HBM)

    index = (block_rows[:, 0, :], block_cols[:, 0, :], counts.T)
    far = pinned(stored)
    near, held, table = pl.pallas_call(
        functools.partial(opening_kernel, grid),
        out_shape=[
            pltpu.VMEM(piece, f32),
            pltpu.VMEM((keep, side, side), stored.dtype),
            pltpu.SMEM((8, slots), jnp.int32),
        ],
        in_specs=[ANY] * 5,
        out_specs=[VMEM, VMEM, SMEM],
        scratch_shapes=[
            pltpu.VMEM((8, slots), jnp.int32),
            *(pltpu.VMEM(x.shape, x.dtype) for x in index),
            pltpu.SemaphoreType.DMA((6,)),
        ],
        compiler_params=limits,
        cost_estimate=cost,
        name="opening",
    )(pinned(start_block), far, *map(pinned, index))
    total = pltpu.VMEM((segment[0] + 1, vectors, side), f32)

    start_row = [near] + along_col([start_block] * (grid_cols - 1))
    (sent,) = product(turned_first, "turned_first", start_row, [chunks], segment[0])
    received = exchange(sent, "row")
    mine, start_gram = product(
        direct_first,
        "direct_first",
        [received, near],
        [segment, square],
        grid_rows * piece_blocks,
        total,
    )
    step = 1
    while True:
        theirs = lax.ppermute(mine, "col", [(i, i ^ step) for i in range(grid_cols)])
        step *= 2
        if step >= grid_cols:
            break
        mine = mine + theirs
    sent, low = product(
        turned_second,
        "turned_second",
        [mine, theirs, start_gram, *start_row],
        [chunks, piece],
        segment[0],
    )
    received = exchange(sent, "row")
    basis, image, inverse = call(
        basis_kernel, "basis", [start_gram, near, low], [piece, piece, square], cost=cost
    )
    own, *rest, grams = product(
        direct_second,
        "direct_second",
        [received, low],
        [piece] * grid_cols + [square],
        grid_rows * piece_blocks,
        total,
    )
    parts = [own] + along_col(rest)
    current, fixed, factor, small, upper = call(
        middle_kernel,
        "middle",
        [grams, basis, image, inverse],
        [piece, piece, square, square, square],
        cost=cost,
    )
    image, local = call(
        functools.partial(second_kernel, grid),
        "second",
        [*parts, current, fixed, factor],
        [piece, (devices, 1, LANES)],
    )
    return call(
        functools.partial(last_kernel, math.sqrt(piece_len * devices)),
        "last",
        [exchange(local, ("row", "col")), current, image, small, upper],
        [piece, (ITERS * vectors, ITERS * vectors)],
    )


def solution(mesh):
    placed = (
        P(None, ("row", "col")),
        P("row", "col", None, None, None),
        P(None, "col", None),
        P(None, "col", None),
        P(),
    )

    def step(*arrays):
        next_block, tridiagonal = jax.shard_map(
            per_device,
            mesh=mesh,
            in_specs=placed,
            out_specs=(P(None, ("row", "col")), P()),
            check_vma=False,
        )(*arrays)
        return next_block, tridiagonal

    return step
```

```python
import functools
import math

import jax
import jax.numpy as jnp
from jax import lax
from jax.experimental import pallas as pl
from jax.experimental.pallas import tpu as pltpu
from jax.sharding import PartitionSpec as P

ITERS = 2
LANES = 128
GROUP = 32
DOWN = 2.0**-2
LOW = 2.0**-4

VMEM = pl.BlockSpec(memory_space=pltpu.VMEM)
SMEM = pl.BlockSpec(memory_space=pltpu.SMEM)
ANY = pl.BlockSpec(memory_space=pl.ANY)
f32 = jnp.float32


def split_terms(x):
    coarse = x.astype(jnp.bfloat16).astype(f32)
    return jnp.concatenate([coarse, x - coarse], axis=0).astype(jnp.bfloat16)


def lane_ids(k):
    return lax.broadcasted_iota(jnp.int32, (k, LANES), 1)


def row_ids(k, width):
    return lax.broadcasted_iota(jnp.int32, (k, width), 0)


def inner(left, right):
    k, width = left.shape
    row, lane = row_ids(k, LANES), lane_ids(k)
    result = jnp.zeros((k, LANES), f32)
    for turn in range(k):
        turned = right if turn == 0 else pltpu.roll(right, turn, 0)
        product = left * turned
        total = product[:, :LANES]
        for low in range(LANES, width, LANES):
            total = total + product[:, low : low + LANES]
        value = jnp.sum(total, axis=1, keepdims=True)
        spot = lane == jnp.where(row >= turn, row - turn, row - turn + k)
        result = jnp.where(spot, value, result)
    return result


def matmul_small(square, tall, transposed=False):
    k, width = tall.shape
    if transposed:
        square = transpose_small(square)
    result = jnp.zeros((k, width), f32)
    for i in range(k):
        result = result + square[:, i : i + 1] * tall[i : i + 1, :]
    return result


def transpose_small(square):
    k = square.shape[0]
    row, lane = row_ids(k, LANES), lane_ids(k)
    result = jnp.zeros((k, LANES), f32)
    for i in range(k):
        line = jnp.sum(
            jnp.where(lane == row_ids(k, LANES), square[:, i : i + 1], 0.0), axis=0, keepdims=True
        )
        result = jnp.where(row == i, line, result)
    return result


def eliminate(gram, tall):
    k, width = tall.shape
    row_small, row_tall = row_ids(k, LANES), row_ids(k, width)
    for i in range(k):
        column = gram[:, i : i + 1]
        scale = 1.0 / jnp.sqrt(gram[i : i + 1, i : i + 1])
        factor = column * scale
        line_small = gram[i : i + 1, :] * scale
        line_tall = tall[i : i + 1, :] * scale
        gram = jnp.where(
            row_small < i,
            gram,
            jnp.where(row_small == i, line_small, gram - factor * line_small),
        )
        tall = jnp.where(
            row_tall < i,
            tall,
            jnp.where(row_tall == i, line_tall, tall - factor * line_tall),
        )
    lane = lane_ids(k)
    upper = jnp.where((lane >= row_small) & (lane < k), gram, 0.0)
    return upper, tall


def own_place():
    return lax.axis_index("row"), lax.axis_index("col")


def opening_kernel(grid, start, blocks, block_rows, block_cols, counts, *refs):
    grid_rows, grid_cols, piece_blocks = grid
    near, held, table, lines, rows_near, cols_near, counts_near, arrived = refs
    r, c = own_place()
    slots = blocks.shape[0]
    pairs = (
        (start, near),
        (block_rows, rows_near),
        (block_cols, cols_near),
        (counts, counts_near),
        (blocks, held),
    )
    moves = [pltpu.make_async_copy(*pair, arrived.at[i]) for i, pair in enumerate(pairs)]
    for move in moves:
        move.start()
    for move in moves[1:4]:
        move.wait()
    block_rows, block_cols, counts = rows_near, cols_near, counts_near
    rids, cids = block_rows[pl.ds(r, 1), :], block_cols[pl.ds(r, 1), :]
    at = (lax.broadcasted_iota(jnp.int32, counts.shape, 0) == c) & (
        lax.broadcasted_iota(jnp.int32, counts.shape, 1) == r
    )
    count = jnp.sum(
        jnp.sum(jnp.where(at, counts[...].astype(f32), 0.0), axis=1, keepdims=True),
        axis=0,
        keepdims=True,
    ).astype(jnp.int32)
    live = lax.broadcasted_iota(jnp.int32, (1, slots), 1) < count
    inside = rids - c * piece_blocks
    same = (inside == cids - r * piece_blocks) & (inside >= 0) & (inside < piece_blocks)
    lines[0:1] = rids
    lines[1:2] = cids
    tile = cids
    for piece in range(1, grid_rows):
        tile = tile + (cids >= piece * piece_blocks).astype(jnp.int32)
    lines[2:3] = jnp.where(live & jnp.logical_not(same), tile, piece_blocks)
    lines[3:4] = jnp.where(live, rids, grid_cols * piece_blocks)
    lines[4:5] = jnp.broadcast_to(count, (1, slots))
    listed = pltpu.make_async_copy(lines, table, arrived.at[5])
    listed.start()
    listed.wait()
    moves[0].wait()
    moves[4].wait()


def each_group(count, held, work):
    for first in range(0, held.shape[0], GROUP):

        @pl.when(first < count)
        def _():
            work(first, [held.at[first + g] for g in range(GROUP)])


def store_pair(total, one, two, y):
    k = y.shape[0] // 4
    side = y.shape[1] // 2
    total[one] += y[:k, :side] + y[k : 2 * k, :side]
    total[two] += y[2 * k : 3 * k, side:] + y[3 * k :, side:]


def turned_products(table, held, taken, sent):
    def work(first, group):
        for g in range(0, GROUP, 2):
            one, two = first + g, first + g + 1
            y = jnp.dot(
                jnp.concatenate([taken[table[0, one]], taken[table[0, two]]], axis=0),
                jnp.concatenate([group[g][...], group[g + 1][...]], axis=1),
                preferred_element_type=f32,
            )
            store_pair(sent, table[2, one], table[2, two], y)

    each_group(table[4, 0], held, work)


def finish_sent(grid, r, sent, own, gram):
    grid_rows, _, piece_blocks = grid
    for piece in range(grid_rows):
        low = piece * (piece_blocks + 1)

        @pl.when(piece > r)
        def _():
            for b in range(piece_blocks):
                sent[low + b] = own[:, b * LANES : (b + 1) * LANES]

        sent[low + piece_blocks] = gram


def turned_first(grid, *refs):
    _, grid_cols, piece_blocks = grid
    table, held = refs[:2]
    pieces = refs[2 : 2 + grid_cols]
    sent, taken = refs[-2:]
    r, c = own_place()
    sent[...] = jnp.zeros_like(sent)
    gram = jnp.zeros(sent.shape[1:], f32)
    for shift in range(grid_cols):
        place = lax.bitwise_xor(c, shift) * piece_blocks
        p = pieces[shift][...]
        for b in range(piece_blocks):
            taken[place + b] = split_terms(p[:, b * LANES : (b + 1) * LANES])
        gram = gram + inner(p, p)
    turned_products(table, held, taken, sent)
    finish_sent(grid, r, sent, pieces[0][...], gram)


def norms_of(gram):
    k = gram.shape[0]
    squares = jnp.sum(jnp.where(lane_ids(k) == row_ids(k, LANES), gram, 0.0), axis=1, keepdims=True)
    return 1.0 / jnp.sqrt(squares)


def turned_second(grid, *refs):
    _, grid_cols, piece_blocks = grid
    table, held, mine, theirs, norms = refs[:5]
    pieces = refs[5 : 5 + grid_cols]
    sent, low_out, taken = refs[-3:]
    r, c = own_place()
    sent[...] = jnp.zeros_like(sent)
    factor = norms[...] * DOWN
    cross = jnp.zeros(sent.shape[1:], f32)
    square = jnp.zeros(sent.shape[1:], f32)
    for shift in range(grid_cols):
        place = lax.bitwise_xor(c, shift) * piece_blocks
        tiles = [(mine[place + b] + theirs[place + b]) * factor for b in range(piece_blocks)]
        for b in range(piece_blocks):
            taken[place + b] = split_terms(tiles[b] * LOW)
        p = jnp.concatenate(tiles, axis=1)
        cross = cross + inner(pieces[shift][...], p)
        square = square + inner(p, p)
        if shift == 0:
            low_out[...] = p * LOW
    turned_products(table, held, taken, sent)
    gram = cross * norms[...] + pltpu.roll(square, square.shape[0], 1)
    finish_sent(grid, r, sent, low_out[...], gram)


def direct_products(grid, table, held, received, own, total, taken):
    grid_rows, _, piece_blocks = grid
    r, _ = own_place()
    tiles = piece_blocks + 1
    for b in range(piece_blocks):
        mine = own[:, b * LANES : (b + 1) * LANES]
        for piece in range(grid_rows):
            x = jnp.where(piece == r, mine, received[piece * tiles + b])
            taken[piece * piece_blocks + b] = split_terms(x)
    total[...] = jnp.zeros_like(total)

    def work(first, group):
        for g in range(0, GROUP, 2):
            one, two = first + g, first + g + 1
            y = lax.dot_general(
                jnp.concatenate([taken[table[1, one]], taken[table[1, two]]], axis=0),
                jnp.concatenate([group[g][...], group[g + 1][...]], axis=0),
                (((1,), (1,)), ((), ())),
                preferred_element_type=f32,
            )
            store_pair(total, table[3, one], table[3, two], y)

    each_group(table[4, 0], held, work)
    part = []
    for b in range(piece_blocks):
        whole = jnp.zeros(total.shape[1:], f32)
        for piece in range(grid_rows):
            whole = whole + jnp.where(piece >= r, received[piece * tiles + b], 0.0)
        part.append(whole)
    grams = received[piece_blocks]
    for piece in range(1, grid_rows):
        grams = grams + received[piece * tiles + piece_blocks]
    return part, grams


def direct_first(grid, *refs):
    _, _, piece_blocks = grid
    out, gram_out, taken, total = refs[-4:]
    _, c = own_place()
    part, gram = direct_products(grid, *refs[:4], total, taken)
    for b in range(piece_blocks):
        total[c * piece_blocks + b] += part[b]
    out[...] = total[: out.shape[0]]
    gram_out[...] = gram


def direct_second(grid, *refs):
    _, grid_cols, piece_blocks = grid
    outs = refs[4 : 4 + grid_cols]
    gram_out, taken, total = refs[-3:]
    _, c = own_place()
    part, gram = direct_products(grid, *refs[:4], total, taken)
    for shift in range(grid_cols):
        place = lax.bitwise_xor(c, shift) * piece_blocks
        for b in range(piece_blocks):
            tile = total[place + b]
            outs[shift][:, b * LANES : (b + 1) * LANES] = tile + part[b] if shift == 0 else tile
    gram_out[...] = gram


def basis_kernel(start_gram, start, basis, inverse, norms_out):
    gram = start_gram[...]
    k, width = start.shape
    same = lane_ids(k) == row_ids(k, LANES)
    norms = norms_of(gram)
    across = jnp.sum(jnp.where(same, norms, 0.0), axis=0, keepdims=True)
    tall = jnp.concatenate([start[...] * norms, same.astype(f32)], axis=1)
    _, solved = eliminate(gram * norms * across, tall)
    basis[...] = solved[:, :width]
    inverse[...] = solved[:, width:]
    norms_out[...] = jnp.broadcast_to(norms, gram.shape)


def middle_kernel(grams_in, basis, low, inverse, current, rest, factor, top, bottom):
    k, width = basis.shape
    lane = lane_ids(k)
    first = inverse[...]
    halves = matmul_small(first, grams_in[...])
    cross = jnp.where(lane < k, halves, 0.0)
    square = jnp.where(lane < k, pltpu.roll(halves, LANES - k, 1), 0.0)
    back = matmul_small(first, transpose_small(cross)) * (1.0 / DOWN)
    squares = matmul_small(first, transpose_small(square)) * (1.0 / DOWN**2)
    projection = transpose_small(back)
    gram = squares - matmul_small(back, projection)
    q1, w1 = basis[...], matmul_small(first, low[...]) * (1.0 / (DOWN * LOW))
    tall = jnp.concatenate(
        [
            w1 - matmul_small(back, q1),
            matmul_small(back * (DOWN * LOW), w1),
            first,
        ],
        axis=1,
    )
    upper, solved = eliminate(gram, tall)
    current[...] = solved[:, :width]
    rest[...] = -(solved[:, width : 2 * width] * (1.0 / (DOWN * LOW))) - matmul_small(upper, q1)
    factor[...] = solved[:, 2 * width :]
    top[...] = jnp.where(lane < k, projection, pltpu.roll(transpose_small(upper), k, 1))
    bottom[...] = upper


def second_kernel(grid, *refs):
    parts = refs[: grid[1]]
    current, rest, factor, image_out, sent = refs[grid[1] :]
    onward = parts[0][...]
    for part in parts[1:]:
        onward = onward + part[...]
    k = onward.shape[0]
    image = matmul_small(factor[...], onward) * (1.0 / (DOWN * LOW)) + rest[...]
    image_out[...] = image
    local = inner(current[...], image) + pltpu.roll(inner(image, image), k, 1)
    line = local[:1]
    for i in range(1, k):
        line = line + pltpu.roll(local[i : i + 1], 2 * k * i, 1)
    sent[...] = jnp.broadcast_to(line[None], sent.shape)


def last_kernel(root, received, current, image_in, top, bottom, out, tri):
    k, width = current.shape
    line = jnp.sum(received[...], axis=0)
    lane = lane_ids(k)
    grams = jnp.concatenate(
        [line] + [pltpu.roll(line, LANES - 2 * k * i, 1) for i in range(1, k)], axis=0
    )
    projection = jnp.where(lane < k, grams, 0.0)
    squares = jnp.where(lane < k, pltpu.roll(grams, LANES - k, 1), 0.0)
    back = transpose_small(projection)
    gram = squares - matmul_small(back, projection)
    image = image_in[...] - matmul_small(back, current[...])
    _, solved = eliminate(gram, image)
    out[...] = solved * root
    lines = jnp.where(lane < k, bottom[...], pltpu.roll(projection, k, 1))
    tri[...] = jnp.concatenate([top[...], lines], axis=0)[:, : 2 * k]


def shapes_of(*shapes):
    return [jax.ShapeDtypeStruct(shape, f32) for shape in shapes]


def per_device(start_block, blocks, block_rows, block_cols, counts):
    vectors, piece_len = start_block.shape
    stored = blocks[0, 0]
    slots, side, _ = stored.shape
    grid_rows, grid_cols = lax.axis_size("row"), lax.axis_size("col")
    piece_blocks = piece_len // side
    grid = (grid_rows, grid_cols, piece_blocks)
    devices = grid_rows * grid_cols
    piece = (vectors, piece_len)
    square = (vectors, LANES)
    chunks = (grid_rows * (piece_blocks + 1), vectors, side)
    segment = (grid_cols * piece_blocks, vectors, side)
    cost = pl.CostEstimate(
        flops=2 * slots * 2 * vectors * side * side,
        bytes_accessed=slots * side * side * 2,
        transcendentals=0,
    )
    limits = pltpu.CompilerParams(vmem_limit_bytes=16 << 20)

    def call(kernel, name, inputs, outs, specs=None, scratch=(), cost=None):
        return pl.pallas_call(
            kernel,
            out_shape=shapes_of(*outs),
            in_specs=(specs or []) + [VMEM] * (len(inputs) - len(specs or [])),
            out_specs=[VMEM] * len(outs),
            scratch_shapes=list(scratch),
            compiler_params=limits,
            cost_estimate=cost,
            name=name,
        )(*inputs)

    def product(kernel, name, inputs, outs, taken_blocks, *total):
        scratch = [
            pltpu.VMEM((taken_blocks, 2 * vectors, side), jnp.bfloat16),
            *total,
        ]
        return call(
            functools.partial(kernel, grid),
            name,
            [table, held, *inputs],
            outs,
            [SMEM, VMEM],
            scratch,
            cost,
        )

    def along_col(parts):
        return [
            lax.ppermute(part, "col", [(i, i ^ s) for i in range(grid_cols)])
            for s, part in enumerate(parts, 1)
        ]

    def exchange(x, axes):
        return lax.all_to_all(x, axes, 0, 0, tiled=True)

    def pinned(x):
        return pltpu.with_memory_space_constraint(x, pltpu.HBM)

    index = (block_rows[:, 0, :], block_cols[:, 0, :], counts.T)
    near, held, table = pl.pallas_call(
        functools.partial(opening_kernel, grid),
        out_shape=[
            pltpu.VMEM(piece, f32),
            pltpu.VMEM(stored.shape, stored.dtype),
            pltpu.SMEM((8, slots), jnp.int32),
        ],
        in_specs=[ANY] * 5,
        out_specs=[VMEM, VMEM, SMEM],
        scratch_shapes=[
            pltpu.VMEM((8, slots), jnp.int32),
            *(pltpu.VMEM(x.shape, x.dtype) for x in index),
            pltpu.SemaphoreType.DMA((6,)),
        ],
        compiler_params=limits,
        cost_estimate=cost,
        name="opening",
    )(pinned(start_block), pinned(stored), *map(pinned, index))
    total = pltpu.VMEM((segment[0] + 1, vectors, side), f32)

    start_row = [near] + along_col([start_block] * (grid_cols - 1))
    (sent,) = product(turned_first, "turned_first", start_row, [chunks], segment[0])
    received = exchange(sent, "row")
    mine, start_gram = product(
        direct_first,
        "direct_first",
        [received, near],
        [segment, square],
        grid_rows * piece_blocks,
        total,
    )
    basis, inverse, norms = call(
        basis_kernel, "basis", [start_gram, near], [piece, square, square], cost=cost
    )
    step = 1
    while True:
        theirs = lax.ppermute(mine, "col", [(i, i ^ step) for i in range(grid_cols)])
        step *= 2
        if step >= grid_cols:
            break
        mine = mine + theirs
    sent, low = product(
        turned_second,
        "turned_second",
        [mine, theirs, norms, *start_row],
        [chunks, piece],
        segment[0],
    )
    received = exchange(sent, "row")
    own, *rest, grams = product(
        direct_second,
        "direct_second",
        [received, low],
        [piece] * grid_cols + [square],
        grid_rows * piece_blocks,
        total,
    )
    parts = [own] + along_col(rest)
    current, fixed, factor, top, bottom = call(
        middle_kernel,
        "middle",
        [grams, basis, low, inverse],
        [piece, piece, square, square, square],
        cost=cost,
    )
    image, local = call(
        functools.partial(second_kernel, grid),
        "second",
        [*parts, current, fixed, factor],
        [piece, (devices, 1, LANES)],
    )
    return call(
        functools.partial(last_kernel, math.sqrt(piece_len * devices)),
        "last",
        [exchange(local, ("row", "col")), current, image, top, bottom],
        [piece, (ITERS * vectors, ITERS * vectors)],
    )


def solution(mesh):
    placed = (
        P(None, ("row", "col")),
        P("row", "col", None, None, None),
        P(None, "col", None),
        P(None, "col", None),
        P(),
    )

    def step(*arrays):
        next_block, tridiagonal = jax.shard_map(
            per_device,
            mesh=mesh,
            in_specs=placed,
            out_specs=(P(None, ("row", "col")), P()),
            check_vma=False,
        )(*arrays)
        return next_block, tridiagonal

    return step
```

```python
import functools
import math

import jax
import jax.numpy as jnp
from jax import lax
from jax.experimental import pallas as pl
from jax.experimental.pallas import tpu as pltpu
from jax.sharding import PartitionSpec as P

ITERS = 2
LANES = 128
DOWN = 2.0**-2
LOW = 2.0**-4

VMEM = pl.BlockSpec(memory_space=pltpu.VMEM)
SMEM = pl.BlockSpec(memory_space=pltpu.SMEM)
ANY = pl.BlockSpec(memory_space=pl.ANY)
f32 = jnp.float32


def split_terms(x):
    coarse = x.astype(jnp.bfloat16).astype(f32)
    return jnp.concatenate([coarse, x - coarse], axis=0).astype(jnp.bfloat16)


def lane_ids(k):
    return lax.broadcasted_iota(jnp.int32, (k, LANES), 1)


def row_ids(k, width):
    return lax.broadcasted_iota(jnp.int32, (k, width), 0)


def inner(left, right):
    k, width = left.shape
    row, lane = row_ids(k, LANES), lane_ids(k)
    result = jnp.zeros((k, LANES), f32)
    for turn in range(k):
        turned = right if turn == 0 else pltpu.roll(right, turn, 0)
        product = left * turned
        total = product[:, :LANES]
        for low in range(LANES, width, LANES):
            total = total + product[:, low : low + LANES]
        value = jnp.sum(total, axis=1, keepdims=True)
        spot = lane == jnp.where(row >= turn, row - turn, row - turn + k)
        result = jnp.where(spot, value, result)
    return result


def matmul_small(square, tall, transposed=False):
    k, width = tall.shape
    if transposed:
        square = transpose_small(square)
    result = jnp.zeros((k, width), f32)
    for i in range(k):
        result = result + square[:, i : i + 1] * tall[i : i + 1, :]
    return result


def transpose_small(square):
    k = square.shape[0]
    row, lane = row_ids(k, LANES), lane_ids(k)
    result = jnp.zeros((k, LANES), f32)
    for i in range(k):
        line = jnp.sum(
            jnp.where(lane == row_ids(k, LANES), square[:, i : i + 1], 0.0), axis=0, keepdims=True
        )
        result = jnp.where(row == i, line, result)
    return result


def eliminate(gram, tall):
    k, width = tall.shape
    row_small, row_tall = row_ids(k, LANES), row_ids(k, width)
    for i in range(k):
        column = gram[:, i : i + 1]
        scale = 1.0 / jnp.sqrt(gram[i : i + 1, i : i + 1])
        factor = column * scale
        line_small = gram[i : i + 1, :] * scale
        line_tall = tall[i : i + 1, :] * scale
        gram = jnp.where(
            row_small < i,
            gram,
            jnp.where(row_small == i, line_small, gram - factor * line_small),
        )
        tall = jnp.where(
            row_tall < i,
            tall,
            jnp.where(row_tall == i, line_tall, tall - factor * line_tall),
        )
    lane = lane_ids(k)
    upper = jnp.where((lane >= row_small) & (lane < k), gram, 0.0)
    return upper, tall


def own_place():
    return lax.axis_index("row"), lax.axis_index("col")


def opening_kernel(grid, start, blocks, block_rows, block_cols, counts, *refs):
    grid_rows, grid_cols, piece_blocks = grid
    near, held, table, lines, rows_near, cols_near, counts_near, arrived = refs
    r, c = own_place()
    slots = blocks.shape[0]
    pairs = (
        (start, near),
        (block_rows, rows_near),
        (block_cols, cols_near),
        (counts, counts_near),
        (blocks, held),
    )
    moves = [pltpu.make_async_copy(*pair, arrived.at[i]) for i, pair in enumerate(pairs)]
    for move in moves:
        move.start()
    for move in moves[1:4]:
        move.wait()
    block_rows, block_cols, counts = rows_near, cols_near, counts_near
    rids, cids = block_rows[pl.ds(r, 1), :], block_cols[pl.ds(r, 1), :]
    at = (lax.broadcasted_iota(jnp.int32, counts.shape, 0) == c) & (
        lax.broadcasted_iota(jnp.int32, counts.shape, 1) == r
    )
    count = jnp.sum(
        jnp.sum(jnp.where(at, counts[...].astype(f32), 0.0), axis=1, keepdims=True),
        axis=0,
        keepdims=True,
    ).astype(jnp.int32)
    live = lax.broadcasted_iota(jnp.int32, (1, slots), 1) < count
    inside = rids - c * piece_blocks
    same = (inside == cids - r * piece_blocks) & (inside >= 0) & (inside < piece_blocks)
    lines[0:1] = rids
    lines[1:2] = cids
    tile = cids
    for piece in range(1, grid_rows):
        tile = tile + (cids >= piece * piece_blocks).astype(jnp.int32)
    lines[2:3] = jnp.where(live & jnp.logical_not(same), tile, piece_blocks)
    lines[3:4] = jnp.where(live, rids, grid_cols * piece_blocks)
    lines[4:] = jnp.zeros((lines.shape[0] - 4, slots), jnp.int32)
    listed = pltpu.make_async_copy(lines, table, arrived.at[5])
    listed.start()
    listed.wait()
    moves[0].wait()
    moves[4].wait()


def store_pair(total, one, two, y):
    k = y.shape[0] // 4
    side = y.shape[1] // 2
    total[one] += y[:k, :side] + y[k : 2 * k, :side]
    total[two] += y[2 * k : 3 * k, side:] + y[3 * k :, side:]


def turned_products(table, held, taken, sent):
    for one in range(0, held.shape[0], 2):
        two = one + 1
        y = jnp.dot(
            jnp.concatenate([taken[table[0, one]], taken[table[0, two]]], axis=0),
            jnp.concatenate([held[one], held[two]], axis=1),
            preferred_element_type=f32,
        )
        store_pair(sent, table[2, one], table[2, two], y)


def finish_sent(grid, r, sent, own, gram):
    grid_rows, _, piece_blocks = grid
    for piece in range(grid_rows):
        low = piece * (piece_blocks + 1)

        @pl.when(piece > r)
        def _():
            for b in range(piece_blocks):
                sent[low + b] = own[:, b * LANES : (b + 1) * LANES]

        sent[low + piece_blocks] = gram


def turned_first(grid, *refs):
    _, grid_cols, piece_blocks = grid
    table, held = refs[:2]
    pieces = refs[2 : 2 + grid_cols]
    sent, taken = refs[-2:]
    r, c = own_place()
    sent[...] = jnp.zeros_like(sent)
    gram = jnp.zeros(sent.shape[1:], f32)
    for shift in range(grid_cols):
        place = lax.bitwise_xor(c, shift) * piece_blocks
        p = pieces[shift][...]
        for b in range(piece_blocks):
            taken[place + b] = split_terms(p[:, b * LANES : (b + 1) * LANES])
        gram = gram + inner(p, p)
    turned_products(table, held, taken, sent)
    finish_sent(grid, r, sent, pieces[0][...], gram)


def norms_of(gram):
    k = gram.shape[0]
    squares = jnp.sum(jnp.where(lane_ids(k) == row_ids(k, LANES), gram, 0.0), axis=1, keepdims=True)
    return 1.0 / jnp.sqrt(squares)


def turned_second(grid, *refs):
    _, grid_cols, piece_blocks = grid
    table, held, mine, theirs, norms = refs[:5]
    pieces = refs[5 : 5 + grid_cols]
    sent, low_out, taken = refs[-3:]
    r, c = own_place()
    sent[...] = jnp.zeros_like(sent)
    factor = norms[...] * DOWN
    cross = jnp.zeros(sent.shape[1:], f32)
    square = jnp.zeros(sent.shape[1:], f32)
    for shift in range(grid_cols):
        place = lax.bitwise_xor(c, shift) * piece_blocks
        tiles = [(mine[place + b] + theirs[place + b]) * factor for b in range(piece_blocks)]
        for b in range(piece_blocks):
            taken[place + b] = split_terms(tiles[b] * LOW)
        p = jnp.concatenate(tiles, axis=1)
        cross = cross + inner(pieces[shift][...], p)
        square = square + inner(p, p)
        if shift == 0:
            low_out[...] = p * LOW
    turned_products(table, held, taken, sent)
    gram = cross * norms[...] + pltpu.roll(square, square.shape[0], 1)
    finish_sent(grid, r, sent, low_out[...], gram)


def direct_products(grid, table, held, received, own, total, taken):
    grid_rows, _, piece_blocks = grid
    r, _ = own_place()
    tiles = piece_blocks + 1
    for b in range(piece_blocks):
        mine = own[:, b * LANES : (b + 1) * LANES]
        for piece in range(grid_rows):
            x = jnp.where(piece == r, mine, received[piece * tiles + b])
            taken[piece * piece_blocks + b] = split_terms(x)
    total[...] = jnp.zeros_like(total)
    for one in range(0, held.shape[0], 2):
        two = one + 1
        y = lax.dot_general(
            jnp.concatenate([taken[table[1, one]], taken[table[1, two]]], axis=0),
            jnp.concatenate([held[one], held[two]], axis=0),
            (((1,), (1,)), ((), ())),
            preferred_element_type=f32,
        )
        store_pair(total, table[3, one], table[3, two], y)
    part = []
    for b in range(piece_blocks):
        whole = jnp.zeros(total.shape[1:], f32)
        for piece in range(grid_rows):
            whole = whole + jnp.where(piece >= r, received[piece * tiles + b], 0.0)
        part.append(whole)
    grams = received[piece_blocks]
    for piece in range(1, grid_rows):
        grams = grams + received[piece * tiles + piece_blocks]
    return part, grams


def direct_first(grid, *refs):
    _, _, piece_blocks = grid
    out, gram_out, taken, total = refs[-4:]
    _, c = own_place()
    part, gram = direct_products(grid, *refs[:4], total, taken)
    for b in range(piece_blocks):
        total[c * piece_blocks + b] += part[b]
    out[...] = total[: out.shape[0]]
    gram_out[...] = gram


def direct_second(grid, *refs):
    _, grid_cols, piece_blocks = grid
    outs = refs[4 : 4 + grid_cols]
    gram_out, taken, total = refs[-3:]
    _, c = own_place()
    part, gram = direct_products(grid, *refs[:4], total, taken)
    for shift in range(grid_cols):
        place = lax.bitwise_xor(c, shift) * piece_blocks
        for b in range(piece_blocks):
            tile = total[place + b]
            outs[shift][:, b * LANES : (b + 1) * LANES] = tile + part[b] if shift == 0 else tile
    gram_out[...] = gram


def basis_kernel(start_gram, start, basis, inverse, norms_out):
    gram = start_gram[...]
    k, width = start.shape
    same = lane_ids(k) == row_ids(k, LANES)
    norms = norms_of(gram)
    across = jnp.sum(jnp.where(same, norms, 0.0), axis=0, keepdims=True)
    tall = jnp.concatenate([start[...] * norms, same.astype(f32)], axis=1)
    _, solved = eliminate(gram * norms * across, tall)
    basis[...] = solved[:, :width]
    inverse[...] = solved[:, width:]
    norms_out[...] = jnp.broadcast_to(norms, gram.shape)


def middle_kernel(grams_in, basis, low, inverse, current, rest, factor, top, bottom):
    k, width = basis.shape
    lane = lane_ids(k)
    first = inverse[...]
    halves = matmul_small(first, grams_in[...])
    cross = jnp.where(lane < k, halves, 0.0)
    square = jnp.where(lane < k, pltpu.roll(halves, LANES - k, 1), 0.0)
    back = matmul_small(first, transpose_small(cross)) * (1.0 / DOWN)
    squares = matmul_small(first, transpose_small(square)) * (1.0 / DOWN**2)
    projection = transpose_small(back)
    gram = squares - matmul_small(back, projection)
    q1, w1 = basis[...], matmul_small(first, low[...]) * (1.0 / (DOWN * LOW))
    tall = jnp.concatenate(
        [
            w1 - matmul_small(back, q1),
            matmul_small(back * (DOWN * LOW), w1),
            first,
        ],
        axis=1,
    )
    upper, solved = eliminate(gram, tall)
    current[...] = solved[:, :width]
    rest[...] = -(solved[:, width : 2 * width] * (1.0 / (DOWN * LOW))) - matmul_small(upper, q1)
    factor[...] = solved[:, 2 * width :]
    top[...] = jnp.where(lane < k, projection, pltpu.roll(transpose_small(upper), k, 1))
    bottom[...] = upper


def second_kernel(grid, *refs):
    parts = refs[: grid[1]]
    current, rest, factor, image_out, sent = refs[grid[1] :]
    onward = parts[0][...]
    for part in parts[1:]:
        onward = onward + part[...]
    k = onward.shape[0]
    image = matmul_small(factor[...], onward) * (1.0 / (DOWN * LOW)) + rest[...]
    image_out[...] = image
    local = inner(current[...], image) + pltpu.roll(inner(image, image), k, 1)
    line = local[:1]
    for i in range(1, k):
        line = line + pltpu.roll(local[i : i + 1], 2 * k * i, 1)
    sent[...] = jnp.broadcast_to(line[None], sent.shape)


def last_kernel(root, received, current, image_in, top, bottom, out, tri):
    k, width = current.shape
    line = jnp.sum(received[...], axis=0)
    lane = lane_ids(k)
    grams = jnp.concatenate(
        [line] + [pltpu.roll(line, LANES - 2 * k * i, 1) for i in range(1, k)], axis=0
    )
    projection = jnp.where(lane < k, grams, 0.0)
    squares = jnp.where(lane < k, pltpu.roll(grams, LANES - k, 1), 0.0)
    back = transpose_small(projection)
    gram = squares - matmul_small(back, projection)
    image = image_in[...] - matmul_small(back, current[...])
    _, solved = eliminate(gram, image)
    out[...] = solved * root
    lines = jnp.where(lane < k, bottom[...], pltpu.roll(projection, k, 1))
    tri[...] = jnp.concatenate([top[...], lines], axis=0)[:, : 2 * k]


def shapes_of(*shapes):
    return [jax.ShapeDtypeStruct(shape, f32) for shape in shapes]


def per_device(start_block, blocks, block_rows, block_cols, counts):
    vectors, piece_len = start_block.shape
    stored = blocks[0, 0]
    slots, side, _ = stored.shape
    grid_rows, grid_cols = lax.axis_size("row"), lax.axis_size("col")
    piece_blocks = piece_len // side
    grid = (grid_rows, grid_cols, piece_blocks)
    devices = grid_rows * grid_cols
    piece = (vectors, piece_len)
    square = (vectors, LANES)
    chunks = (grid_rows * (piece_blocks + 1), vectors, side)
    segment = (grid_cols * piece_blocks, vectors, side)
    cost = pl.CostEstimate(
        flops=2 * slots * 2 * vectors * side * side,
        bytes_accessed=slots * side * side * 2,
        transcendentals=0,
    )
    limits = pltpu.CompilerParams(vmem_limit_bytes=16 << 20)

    def call(kernel, name, inputs, outs, specs=None, scratch=(), cost=None):
        return pl.pallas_call(
            kernel,
            out_shape=shapes_of(*outs),
            in_specs=(specs or []) + [VMEM] * (len(inputs) - len(specs or [])),
            out_specs=[VMEM] * len(outs),
            scratch_shapes=list(scratch),
            compiler_params=limits,
            cost_estimate=cost,
            name=name,
        )(*inputs)

    def product(kernel, name, inputs, outs, taken_blocks, *total):
        scratch = [
            pltpu.VMEM((taken_blocks, 2 * vectors, side), jnp.bfloat16),
            *total,
        ]
        return call(
            functools.partial(kernel, grid),
            name,
            [table, held, *inputs],
            outs,
            [SMEM, VMEM],
            scratch,
            cost,
        )

    def along_col(parts):
        return [
            lax.ppermute(part, "col", [(i, i ^ s) for i in range(grid_cols)])
            for s, part in enumerate(parts, 1)
        ]

    def exchange(x, axes):
        return lax.all_to_all(x, axes, 0, 0, tiled=True)

    def pinned(x):
        return pltpu.with_memory_space_constraint(x, pltpu.HBM)

    index = (block_rows[:, 0, :], block_cols[:, 0, :], counts.T)
    near, held, table = pl.pallas_call(
        functools.partial(opening_kernel, grid),
        out_shape=[
            pltpu.VMEM(piece, f32),
            pltpu.VMEM(stored.shape, stored.dtype),
            pltpu.SMEM((8, slots), jnp.int32),
        ],
        in_specs=[ANY] * 5,
        out_specs=[VMEM, VMEM, SMEM],
        scratch_shapes=[
            pltpu.VMEM((8, slots), jnp.int32),
            *(pltpu.VMEM(x.shape, x.dtype) for x in index),
            pltpu.SemaphoreType.DMA((6,)),
        ],
        compiler_params=limits,
        cost_estimate=cost,
        name="opening",
    )(pinned(start_block), pinned(stored), *map(pinned, index))
    total = pltpu.VMEM((segment[0] + 1, vectors, side), f32)

    start_row = [near] + along_col([start_block] * (grid_cols - 1))
    (sent,) = product(turned_first, "turned_first", start_row, [chunks], segment[0])
    received = exchange(sent, "row")
    mine, start_gram = product(
        direct_first,
        "direct_first",
        [received, near],
        [segment, square],
        grid_rows * piece_blocks,
        total,
    )
    basis, inverse, norms = call(
        basis_kernel, "basis", [start_gram, near], [piece, square, square], cost=cost
    )
    step = 1
    while True:
        theirs = lax.ppermute(mine, "col", [(i, i ^ step) for i in range(grid_cols)])
        step *= 2
        if step >= grid_cols:
            break
        mine = mine + theirs
    sent, low = product(
        turned_second,
        "turned_second",
        [mine, theirs, norms, *start_row],
        [chunks, piece],
        segment[0],
    )
    received = exchange(sent, "row")
    own, *rest, grams = product(
        direct_second,
        "direct_second",
        [received, low],
        [piece] * grid_cols + [square],
        grid_rows * piece_blocks,
        total,
    )
    parts = [own] + along_col(rest)
    current, fixed, factor, top, bottom = call(
        middle_kernel,
        "middle",
        [grams, basis, low, inverse],
        [piece, piece, square, square, square],
        cost=cost,
    )
    image, local = call(
        functools.partial(second_kernel, grid),
        "second",
        [*parts, current, fixed, factor],
        [piece, (devices, 1, LANES)],
    )
    return call(
        functools.partial(last_kernel, math.sqrt(piece_len * devices)),
        "last",
        [exchange(local, ("row", "col")), current, image, top, bottom],
        [piece, (ITERS * vectors, ITERS * vectors)],
    )


def solution(mesh):
    placed = (
        P(None, ("row", "col")),
        P("row", "col", None, None, None),
        P(None, "col", None),
        P(None, "col", None),
        P(),
    )

    def step(*arrays):
        next_block, tridiagonal = jax.shard_map(
            per_device,
            mesh=mesh,
            in_specs=placed,
            out_specs=(P(None, ("row", "col")), P()),
            check_vma=False,
        )(*arrays)
        return next_block, tridiagonal

    return step
```
